256 devices in a mesh: seq: 32 (over y, z), ch: 8 (over x, core).
Axes of the slice: x: 4, y: 4, z: 8, core: 2. Of those that a mesh axis runs over, the one named last changes fastest.
Arguments:
- query_input: bfloat16 [4096, 4096], P('seq', 'ch'), may hold values from -6 to 6
- key_input: bfloat16 [4096, 4096], P('seq', 'ch'), may hold values from -6 to 6
- value_input: bfloat16 [4096, 4096], P('seq', 'ch'), may hold values from -6 to 6
- cotangent: bfloat16 [4096, 4096], P('seq', 'ch'), may hold values from -6 to 6
- filter_taps: float32 [4096, 4096], P('seq', 'ch'), may hold values from -0.09375 to 0.09375
- skip_gain: float32 [4096], P('ch'), may hold values from -2 to 2
Outputs:
- output: bfloat16 [4096, 4096], P('seq', 'ch')
- query_grad: bfloat16 [4096, 4096], P('seq', 'ch')
- key_grad: bfloat16 [4096, 4096], P('seq', 'ch')
- value_grad: bfloat16 [4096, 4096], P('seq', 'ch')
- filter_grad: float32 [4096, 4096], P('seq', 'ch')
- skip_grad: float32 [4096], P('ch')
- grad_rms: float32 [], replicated
The draws below stay inside these ranges and needn't reach their ends.
All inputs are finite; a program needn't handle non-finite values.
Results may differ from the reference program's by a relative error of at most 0.0014.
Values sent between devices are 32-bit elements; how exact they have to be, the bound alone decides.
No kernel may reach another device: no remote copies, remote signals or barrier semaphores. Data moves between devices by JAX's collectives and lax.ppermute only.
A program may use at most 64 MiB of HBM per device.

```python
import math
import jax
import jax.numpy as jnp
from jax import lax

CH_DEV = 512
TOKENS = 4096
CHANNELS = 4096
N_CH = 8


def level_of(own_key, dims, cuts, least, top_value):
    loudness = 1.0
    for dim, parts in cuts:
        heights = jax.random.uniform(jax.random.fold_in(jax.random.fold_in(own_key, 6), dim), (parts,), jnp.float32, least / len(cuts), top_value / len(cuts))
        loudness = loudness * jnp.repeat(jnp.exp(heights), dims[dim] // parts).reshape((-1,) + (1,) * (len(dims) - 1 - dim))
    return loudness


def gaussian(key, dims, deviation, reach, pieces=(), held_as=jnp.bfloat16):
    entries = deviation * jax.random.normal(key, dims, jnp.float32)
    if pieces:
        entries = entries * level_of(key, dims, pieces, -0.22, 0.18)
    return jnp.clip(entries, -reach, reach).astype(held_as)


def setup_inputs(seed: int = 0) -> dict:
    splits = jax.random.split(jax.random.key(seed), 7)
    return {
        "query_input": gaussian(splits[0], (TOKENS, CHANNELS), 1.0, 6.0, ((0, 32), (1, 8))),
        "key_input": gaussian(splits[1], (TOKENS, CHANNELS), 1.0, 6.0, ((0, 32), (1, 8))),
        "value_input": gaussian(splits[2], (TOKENS, CHANNELS), 1.0, 6.0, ((0, 32), (1, 8))),
        "cotangent": gaussian(splits[3], (TOKENS, CHANNELS), 1.0, 6.0, ((0, 32), (1, 8))),
        "filter_taps": gaussian(splits[4], (TOKENS, CHANNELS), TOKENS ** -0.5, 0.09375, ((0, 32), (1, 8)), jnp.float32),
        "skip_gain": gaussian(splits[5], (CHANNELS,), 0.5, 2.0, ((0, 8),), jnp.float32),
    }


def one_group(operands):
    query_input, key_input, value_input, cotangent, filter_taps, skip_gain = operands
    query_val = query_input.astype(jnp.float32)
    key_val = key_input.astype(jnp.float32)
    value_val = value_input.astype(jnp.float32)
    cot_val = cotangent.astype(jnp.float32)
    mixed_in = key_val * value_val
    gated_cot = query_val * cot_val
    length = 2 * TOKENS
    mixed_spec = jnp.fft.rfft(mixed_in, n=length, axis=0)
    gated_spec = jnp.fft.rfft(gated_cot, n=length, axis=0)
    taps_spec = jnp.fft.rfft(filter_taps, n=length, axis=0)
    conv_out = jnp.fft.irfft(mixed_spec * taps_spec, n=length, axis=0)[:TOKENS]
    back_conv = jnp.fft.irfft(gated_spec * jnp.conj(taps_spec), n=length, axis=0)[:TOKENS]
    kernel_grad = jnp.fft.irfft(gated_spec * jnp.conj(mixed_spec), n=length, axis=0)[:TOKENS]
    inner_sum = conv_out + skip_gain[None, :] * mixed_in
    mixed_grad = back_conv + skip_gain[None, :] * gated_cot
    grad_scale = 1.0 / math.sqrt(TOKENS)
    return ((query_val * inner_sum).astype(jnp.bfloat16), (cot_val * inner_sum).astype(jnp.bfloat16), (mixed_grad * value_val).astype(jnp.bfloat16), (mixed_grad * key_val).astype(jnp.bfloat16), kernel_grad * grad_scale, lax.optimization_barrier(jnp.sum(gated_cot * mixed_in, axis=0)) * grad_scale)

def split_rows(array):
    return jnp.moveaxis(array.reshape(array.shape[0], N_CH, CH_DEV), 1, 0)

def join_rows(array):
    return jnp.moveaxis(array, 0, 1).reshape(array.shape[1], N_CH * CH_DEV)

def reference(query_input, key_input, value_input, cotangent, filter_taps, skip_gain):
    operands = (split_rows(query_input), split_rows(key_input), split_rows(value_input), split_rows(cotangent), split_rows(filter_taps), skip_gain.reshape(N_CH, CH_DEV))
    results = lax.map(one_group, operands)
    output = join_rows(results[0])
    query_grad = join_rows(results[1])
    key_grad = join_rows(results[2])
    value_grad = join_rows(results[3])
    filter_grad = join_rows(results[4])
    skip_grad = results[5].reshape(CHANNELS)
    squares = jnp.sum(filter_grad * filter_grad) + jnp.sum(skip_grad * skip_grad)
    grad_rms = jnp.sqrt(squares / (CHANNELS * (TOKENS + 1)))
    return (output, query_grad, key_grad, value_grad, filter_grad, skip_grad, grad_rms)
```

```python
import math

import jax
import jax.numpy as jnp
import numpy as np
from jax import lax
from jax.experimental import pallas as pl
from jax.experimental.pallas import tpu as pltpu
from jax.sharding import PartitionSpec as P

ROWS = 128
BLOCKS = 32
LENGTH = ROWS * BLOCKS
CH_EACH = 16
LINES = 3 * CH_EACH
GROUP = 8


def tables():
    n2 = np.arange(ROWS)
    k1 = np.arange(BLOCKS)
    angle = 2.0 * np.pi * n2[None, :] * (k1[:, None] + 0.25) / LENGTH
    twiddle = np.stack([np.cos(angle), -np.sin(angle)]).astype(np.float32)
    angle = 2.0 * np.pi * ((n2[:, None] * n2[None, :]) % ROWS) / ROWS
    cosine, sine = np.cos(angle), np.sin(angle)
    whole = np.block([[cosine, -sine], [sine, cosine]]).astype(np.float32)
    high = whole.astype(jnp.bfloat16)
    low = (whole - high.astype(np.float32)).astype(jnp.bfloat16)
    return twiddle, np.stack([high, low])


def times(value, angle):
    re, im = value
    turn = round(angle / (math.pi / 4), 9) % 8
    half = math.sqrt(0.5)
    if turn == 0:
        return re, im
    if turn == 2:
        return im, -re
    if turn == 1:
        return (re + im) * half, (im - re) * half
    if turn == 3:
        return (im - re) * half, -(re + im) * half
    c, s = math.cos(angle), math.sin(angle)
    return re * c + im * s, im * c - re * s


def add(a, b):
    return a[0] + b[0], a[1] + b[1]


def sub(a, b):
    return a[0] - b[0], a[1] - b[1]


def split_radix(values):
    count = len(values)
    if count == 1:
        return values
    if count == 2:
        return [add(*values), sub(*values)]
    even = split_radix(values[0::2])
    first = split_radix(values[1::4])
    third = split_radix(values[3::4])
    quarter = count // 4
    out = [None] * count
    for k in range(quarter):
        one = times(first[k], 2 * math.pi * k / count)
        two = times(third[k], 2 * math.pi * 3 * k / count)
        total, diff = add(one, two), sub(one, two)
        out[k] = add(even[k], total)
        out[k + 2 * quarter] = sub(even[k], total)
        e_re, e_im = even[k + quarter]
        out[k + quarter] = (e_re + diff[1], e_im - diff[0])
        out[k + 3 * quarter] = (e_re - diff[1], e_im + diff[0])
    return out


def pre_kernel(q_ref, k_ref, v_ref, cot_ref, taps_ref, out_ref, skip_ref):
    mixed = k_ref[...].astype(jnp.float32) * v_ref[...].astype(jnp.float32)
    gated = q_ref[...].astype(jnp.float32) * cot_ref[...].astype(jnp.float32)
    skip_ref[...] = jnp.sum(mixed * gated, axis=0, keepdims=True)
    for index, signal in enumerate((mixed, gated, taps_ref[...])):
        lines = signal.T.reshape(BLOCKS, CH_EACH, ROWS)
        out_ref[:, index * CH_EACH : (index + 1) * CH_EACH, :] = lines


def split(value):
    high = value.astype(jnp.bfloat16)
    low = (value - high.astype(jnp.float32)).astype(jnp.bfloat16)
    return high, low


def dft_rows(value, mat_ref):
    high, low = split(value)

    def dot(left, right):
        return jnp.dot(left, right, preferred_element_type=jnp.float32)

    return dot(high, mat_ref[0]) + (dot(low, mat_ref[0]) + dot(high, mat_ref[1]))


def main_kernel(in_ref, tw_ref, mat_ref, out_ref, sq_ref, mid_ref):
    @pl.loop(0, LINES // 8)
    def _(step):
        lines = pl.ds(pl.multiple_of(step * 8, 8), 8)
        values = []
        for s in range(BLOCKS):
            signal = in_ref[s, lines, :]
            angle = 2 * math.pi * s / (4 * BLOCKS)
            values.append((signal * math.cos(angle), signal * -math.sin(angle)))
        for k1, (re, im) in enumerate(split_radix(values)):
            t_re, t_im = tw_ref[0, k1 : k1 + 1, :], tw_ref[1, k1 : k1 + 1, :]
            mid_ref[k1, lines, :ROWS] = re * t_re - im * t_im
            mid_ref[k1, lines, ROWS:] = re * t_im + im * t_re

    @pl.loop(0, BLOCKS // GROUP)
    def _(step):
        first = pl.multiple_of(step * GROUP, GROUP)
        here = pl.ds(first, GROUP)
        held = mid_ref[here].reshape(GROUP * LINES, 2 * ROWS)
        spectrum = dft_rows(held, mat_ref).reshape(GROUP, LINES, 2 * ROWS)
        re, im = spectrum[:, :, :ROWS], spectrum[:, :, ROWS:]
        x_re, g_re, h_re = (re[:, i * CH_EACH : (i + 1) * CH_EACH] for i in range(3))
        x_im, g_im, h_im = (im[:, i * CH_EACH : (i + 1) * CH_EACH] for i in range(3))
        product = jnp.concatenate(
            [
                jnp.concatenate([x_re * h_re - x_im * h_im, -(x_re * h_im + x_im * h_re)], axis=2),
                jnp.concatenate([g_re * h_re + g_im * h_im, g_re * h_im - g_im * h_re], axis=2),
                jnp.concatenate([g_re * x_re + g_im * x_im, g_re * x_im - g_im * x_re], axis=2),
            ],
            axis=1,
        )
        back = dft_rows(product.reshape(GROUP * LINES, 2 * ROWS), mat_ref)
        back = back.reshape(GROUP, LINES, 2 * ROWS)
        re, im = back[:, :, :ROWS], back[:, :, ROWS:]
        t_re, t_im = tw_ref[0, here, :][:, None, :], tw_ref[1, here, :][:, None, :]
        mid_ref[here, :, :ROWS] = re * t_re - im * t_im
        mid_ref[here, :, ROWS:] = re * t_im + im * t_re

    squares = jnp.zeros((8, ROWS), jnp.float32)
    for index in range(3):
        scale = 1.0 / LENGTH if index < 2 else 1.0 / LENGTH / math.sqrt(LENGTH)
        for half in range(CH_EACH // 8):
            line = index * CH_EACH + half * 8
            lines = slice(line, line + 8)
            values = [
                (mid_ref[k1, lines, :ROWS], mid_ref[k1, lines, ROWS:]) for k1 in range(BLOCKS)
            ]
            for s, (re, im) in enumerate(split_radix(values)):
                angle = 2 * math.pi * s / (4 * BLOCKS)
                series = re * (math.cos(angle) * scale) + im * (math.sin(angle) * scale)
                out_ref[s, lines, :] = series
                if index == 2:
                    squares = squares + series * series
    sq_ref[...] = squares


def post_kernel(
    in_ref, q_ref, k_ref, v_ref, cot_ref, gain_ref, out_ref, dq_ref, dk_ref, dv_ref, dh_ref
):
    def series(index):
        lines = in_ref[:, index * CH_EACH : (index + 1) * CH_EACH, :]
        return lines.reshape(BLOCKS * CH_EACH, ROWS).T

    query = q_ref[...].astype(jnp.float32)
    key = k_ref[...].astype(jnp.float32)
    value = v_ref[...].astype(jnp.float32)
    cot = cot_ref[...].astype(jnp.float32)
    gain = gain_ref[...]
    inner = series(0) + gain * (key * value)
    out_ref[...] = (query * inner).astype(jnp.bfloat16)
    dq_ref[...] = (cot * inner).astype(jnp.bfloat16)
    mixed_grad = series(1) + gain * (query * cot)
    dk_ref[...] = (mixed_grad * value).astype(jnp.bfloat16)
    dv_ref[...] = (mixed_grad * key).astype(jnp.bfloat16)
    dh_ref[...] = series(2)


def everyone(array, axis, bits):
    count = lax.axis_size(axis)
    for bit in bits:
        array = array + lax.ppermute(array, axis, [(i, i ^ bit) for i in range(count)])
    return array


def f32(*shape):
    return jax.ShapeDtypeStruct(shape, jnp.float32)


PARAMS = pltpu.CompilerParams(vmem_limit_bytes=40 * 2**20)


def body(query, key, value, cotangent, taps, gain):
    rows, channels = query.shape
    twiddle, matrix = tables()
    packed, skip_part = pl.pallas_call(
        pre_kernel,
        out_shape=(f32(BLOCKS, LINES, ROWS), f32(1, channels)),
        compiler_params=PARAMS,
    )(query, key, value, cotangent, taps)
    packed = lax.all_to_all(packed, "seq", 0, 0, tiled=True)
    time_scale = 1.0 / math.sqrt(LENGTH)
    skip_grad = everyone(skip_part, "seq", (1, 2, 4, 8, 16))[0] * time_scale
    results, squares = pl.pallas_call(
        main_kernel,
        out_shape=(f32(BLOCKS, LINES, ROWS), f32(8, ROWS)),
        scratch_shapes=[pltpu.VMEM((BLOCKS, LINES, 2 * ROWS), jnp.float32)],
        compiler_params=PARAMS,
    )(packed, twiddle, matrix)
    results = lax.all_to_all(results, "seq", 0, 0, tiled=True)
    total = jnp.sum(everyone(squares, "seq", (1, 2, 4, 8, 16))) + jnp.sum(skip_grad * skip_grad)
    total = everyone(total[None], "ch", (1, 2, 4))[0]
    grad_rms = jnp.sqrt(total / (channels * lax.axis_size("ch") * (LENGTH + 1)))
    bf16 = jax.ShapeDtypeStruct((rows, channels), jnp.bfloat16)
    output, query_grad, key_grad, value_grad, filter_grad = pl.pallas_call(
        post_kernel,
        out_shape=(bf16, bf16, bf16, bf16, f32(rows, channels)),
        compiler_params=PARAMS,
    )(results, query, key, value, cotangent, gain[None, :])
    return output, query_grad, key_grad, value_grad, filter_grad, skip_grad, grad_rms


def solution(mesh):
    both = P("seq", "ch")
    return jax.shard_map(
        body,
        mesh=mesh,
        in_specs=(both, both, both, both, both, P("ch")),
        out_specs=(both, both, both, both, both, P("ch"), P()),
        check_vma=False,
    )
```

```python
import math

import jax
import jax.numpy as jnp
import numpy as np
from jax import lax
from jax.experimental import pallas as pl
from jax.experimental.pallas import tpu as pltpu
from jax.sharding import PartitionSpec as P

ROWS = 128
BLOCKS = 32
LENGTH = ROWS * BLOCKS
CH_EACH = 16
LINES = 3 * CH_EACH
GROUP = 8
BACK = LINES + 1
ORDER = list(range(BLOCKS))
PLACE = [ORDER.index(s) for s in range(BLOCKS)]


def tables():
    n2 = np.arange(ROWS)
    k1 = np.arange(BLOCKS)
    angle = 2.0 * np.pi * n2[None, :] * (k1[:, None] + 0.25) / LENGTH
    twiddle = np.stack([np.cos(angle), -np.sin(angle)]).astype(np.float32)
    angle = 2.0 * np.pi * ((n2[:, None] * n2[None, :]) % ROWS) / ROWS
    cosine, sine = np.cos(angle), np.sin(angle)
    whole = np.block([[cosine, -sine], [sine, cosine]]).astype(np.float32)
    high = whole.astype(jnp.bfloat16)
    low = (whole - high.astype(np.float32)).astype(jnp.bfloat16)
    return twiddle, np.stack([high, low])


def times(value, angle):
    re, im = value
    turn = round(angle / (math.pi / 4), 9) % 8
    half = math.sqrt(0.5)
    if turn == 0:
        return re, im
    if turn == 2:
        return im, -re
    if turn == 1:
        return (re + im) * half, (im - re) * half
    if turn == 3:
        return (im - re) * half, -(re + im) * half
    c, s = math.cos(angle), math.sin(angle)
    return re * c + im * s, im * c - re * s


def add(a, b):
    return a[0] + b[0], a[1] + b[1]


def sub(a, b):
    return a[0] - b[0], a[1] - b[1]


def split_radix(values):
    count = len(values)
    if count == 1:
        return values
    if count == 2:
        return [add(*values), sub(*values)]
    even = split_radix(values[0::2])
    first = split_radix(values[1::4])
    third = split_radix(values[3::4])
    quarter = count // 4
    out = [None] * count
    for k in range(quarter):
        one = times(first[k], 2 * math.pi * k / count)
        two = times(third[k], 2 * math.pi * 3 * k / count)
        total, diff = add(one, two), sub(one, two)
        out[k] = add(even[k], total)
        out[k + 2 * quarter] = sub(even[k], total)
        e_re, e_im = even[k + quarter]
        out[k + quarter] = (e_re + diff[1], e_im - diff[0])
        out[k + 3 * quarter] = (e_re - diff[1], e_im + diff[0])
    return out


def pre_kernel(q_hbm, k_hbm, v_hbm, cot_hbm, taps_hbm, out_hbm, *scratch):
    buffers, out_ref, in_sems, out_sems = scratch[:5], *scratch[5:]
    sources = (q_hbm, k_hbm, v_hbm, cot_hbm, taps_hbm)
    loads = [pltpu.make_async_copy(sources[i], buffers[i], in_sems.at[i]) for i in range(5)]
    for i in (4, 1, 2, 0, 3):
        loads[i].start()
    stores = []
    for index, needs in ((2, (4,)), (0, (1, 2)), (1, (0, 3))):
        signal = None
        for i in needs:
            loads[i].wait()
            factor = buffers[i][...].astype(jnp.float32)
            signal = factor if signal is None else signal * factor
        lines = signal.T.reshape(BLOCKS, CH_EACH, ROWS)
        for s in range(BLOCKS):
            out_ref[index, PLACE[s]] = lines[s]
        here = slice(index * CH_EACH, (index + 1) * CH_EACH)
        store = pltpu.make_async_copy(
            out_ref.at[index], out_hbm.at[:, here, :], out_sems.at[index]
        )
        store.start()
        stores.append(store)
    for store in stores:
        store.wait()


def split(value):
    high = value.astype(jnp.bfloat16)
    low = (value - high.astype(jnp.float32)).astype(jnp.bfloat16)
    return high, low


def dft_rows(value, mat_ref):
    high, low = split(value)

    def dot(left, right):
        return jnp.dot(left, right, preferred_element_type=jnp.float32)

    return dot(high, mat_ref[0]) + (dot(low, mat_ref[0]) + dot(high, mat_ref[1]))


def main_kernel(in_ref, tw_ref, mat_ref, out_ref, mid_ref):
    @pl.loop(0, LINES // 8)
    def _(step):
        lines = pl.ds(pl.multiple_of(step * 8, 8), 8)
        values = []
        for s in range(BLOCKS):
            signal = in_ref[PLACE[s], lines, :]
            angle = 2 * math.pi * s / (4 * BLOCKS)
            values.append((signal * math.cos(angle), signal * -math.sin(angle)))
        for k1, (re, im) in enumerate(split_radix(values)):
            t_re, t_im = tw_ref[0, k1 : k1 + 1, :], tw_ref[1, k1 : k1 + 1, :]
            mid_ref[k1, lines, :ROWS] = re * t_re - im * t_im
            mid_ref[k1, lines, ROWS:] = re * t_im + im * t_re

    @pl.loop(0, BLOCKS // GROUP)
    def _(step):
        first = pl.multiple_of(step * GROUP, GROUP)
        here = pl.ds(first, GROUP)
        held = mid_ref[here].reshape(GROUP * LINES, 2 * ROWS)
        spectrum = dft_rows(held, mat_ref).reshape(GROUP, LINES, 2 * ROWS)
        re, im = spectrum[:, :, :ROWS], spectrum[:, :, ROWS:]
        x_re, g_re, h_re = (re[:, i * CH_EACH : (i + 1) * CH_EACH] for i in range(3))
        x_im, g_im, h_im = (im[:, i * CH_EACH : (i + 1) * CH_EACH] for i in range(3))
        product = jnp.concatenate(
            [
                jnp.concatenate([x_re * h_re - x_im * h_im, -(x_re * h_im + x_im * h_re)], axis=2),
                jnp.concatenate([g_re * h_re + g_im * h_im, g_re * h_im - g_im * h_re], axis=2),
                jnp.concatenate([g_re * x_re + g_im * x_im, g_re * x_im - g_im * x_re], axis=2),
            ],
            axis=1,
        )
        back = dft_rows(product.reshape(GROUP * LINES, 2 * ROWS), mat_ref)
        back = back.reshape(GROUP, LINES, 2 * ROWS)
        re, im = back[:, :, :ROWS], back[:, :, ROWS:]
        t_re, t_im = tw_ref[0, here, :][:, None, :], tw_ref[1, here, :][:, None, :]
        mid_ref[here, :, :ROWS] = re * t_re - im * t_im
        mid_ref[here, :, ROWS:] = re * t_im + im * t_re

    squares = jnp.zeros((8, ROWS), jnp.float32)
    for index in range(3):
        scale = 1.0 / LENGTH if index < 2 else 1.0 / LENGTH / math.sqrt(LENGTH)
        for half in range(CH_EACH // 8):
            line = index * CH_EACH + half * 8
            lines = slice(line, line + 8)
            values = [
                (mid_ref[k1, lines, :ROWS], mid_ref[k1, lines, ROWS:]) for k1 in range(BLOCKS)
            ]
            for s, (re, im) in enumerate(split_radix(values)):
                angle = 2 * math.pi * s / (4 * BLOCKS)
                series = re * (math.cos(angle) * scale) + im * (math.sin(angle) * scale)
                out_ref[PLACE[s] * BACK + line : PLACE[s] * BACK + line + 8, :] = series
                if index == 2:
                    squares = squares + series * series

    direct = jnp.zeros((CH_EACH, ROWS), jnp.float32)
    for s in range(BLOCKS):
        direct = direct + in_ref[s, :CH_EACH, :] * in_ref[s, CH_EACH : 2 * CH_EACH, :]
    direct = jnp.sum(direct, axis=1, keepdims=True) * (1.0 / math.sqrt(LENGTH))
    row = lax.broadcasted_iota(jnp.int32, (CH_EACH, ROWS), 0)
    lane = lax.broadcasted_iota(jnp.int32, (CH_EACH, ROWS), 1)
    last = jnp.sum(jnp.where(row == lane, direct, 0.0), axis=0, keepdims=True)
    squares = jnp.sum(jnp.sum(squares, axis=0, keepdims=True), axis=1, keepdims=True)
    last = jnp.where(lane[:1] == CH_EACH, squares, last)
    for s in range(BLOCKS):
        out_ref[s * BACK + LINES : (s + 1) * BACK, :] = last


def stats_kernel(in_ref, skip_ref, sum_ref):
    per_row = ROWS // CH_EACH
    rows = BLOCKS // per_row
    lane = lax.broadcasted_iota(jnp.int32, (rows, ROWS), 1)
    skip = jnp.zeros((rows, ROWS), jnp.float32)
    squares = jnp.zeros((rows, ROWS), jnp.float32)
    for m in range(per_row):
        at = [PLACE[r * per_row + m] * BACK + LINES for r in range(rows)]
        lines = jnp.concatenate([in_ref[i : i + 1, :] for i in at], axis=0)
        squares = squares + jnp.where(lane == CH_EACH, lines, 0.0)
        moved = pltpu.roll(lines, m * CH_EACH, 1) if m else lines
        skip = jnp.where(lane // CH_EACH == m, moved, skip)
    skip_ref[...] = skip
    sum_ref[...] = jnp.sum(squares + skip * skip, axis=0, keepdims=True)


def post_kernel(
    in_ref, q_ref, k_ref, v_ref, cot_ref, gain_ref, out_ref, dq_ref, dk_ref, dv_ref, dh_ref
):
    def series(index):
        first = [PLACE[s] * BACK + index * CH_EACH for s in range(BLOCKS)]
        return jnp.concatenate([in_ref[i : i + CH_EACH, :] for i in first], axis=0).T

    query = q_ref[...].astype(jnp.float32)
    key = k_ref[...].astype(jnp.float32)
    value = v_ref[...].astype(jnp.float32)
    cot = cot_ref[...].astype(jnp.float32)
    gain = gain_ref[...]
    inner = series(0) + gain * (key * value)
    out_ref[...] = (query * inner).astype(jnp.bfloat16)
    dq_ref[...] = (cot * inner).astype(jnp.bfloat16)
    mixed_grad = series(1) + gain * (query * cot)
    dk_ref[...] = (mixed_grad * value).astype(jnp.bfloat16)
    dv_ref[...] = (mixed_grad * key).astype(jnp.bfloat16)
    dh_ref[...] = series(2)


def partner(array, bit):
    return lax.ppermute(array, "ch", [(i, i ^ bit) for i in range(lax.axis_size("ch"))])


def over_channels(array):
    array = array + partner(array, 1)
    two, four, six = (partner(array, bit) for bit in (2, 4, 6))
    return (array + two) + (four + six)


def exchange(array):
    return lax.all_to_all(array, "seq", 0, 0, axis_index_groups=[ORDER], tiled=True)


def f32(*shape):
    return jax.ShapeDtypeStruct(shape, jnp.float32)


PARAMS = pltpu.CompilerParams(vmem_limit_bytes=40 * 2**20)
WIDE = pltpu.CompilerParams(vmem_limit_bytes=60 * 2**20)


def body(query, key, value, cotangent, taps, gain):
    rows, channels = query.shape
    twiddle, matrix = tables()
    signals = (query, key, value, cotangent, taps)
    hbm = pl.BlockSpec(memory_space=pltpu.HBM)
    packed = pl.pallas_call(
        pre_kernel,
        out_shape=f32(BLOCKS, LINES, ROWS),
        in_specs=[hbm] * len(signals),
        out_specs=hbm,
        scratch_shapes=[pltpu.VMEM(signal.shape, signal.dtype) for signal in signals]
        + [
            pltpu.VMEM((3, BLOCKS, CH_EACH, ROWS), jnp.float32),
            pltpu.SemaphoreType.DMA((len(signals),)),
            pltpu.SemaphoreType.DMA((3,)),
        ],
        compiler_params=WIDE,
    )(*signals)
    results = pl.pallas_call(
        main_kernel,
        out_shape=f32(BLOCKS * BACK, ROWS),
        scratch_shapes=[pltpu.VMEM((BLOCKS, LINES, 2 * ROWS), jnp.float32)],
        compiler_params=PARAMS,
    )(exchange(packed), twiddle, matrix)
    results = exchange(results.reshape(BLOCKS, BACK, 1, ROWS)).reshape(BLOCKS * BACK, ROWS)
    skip_grad, total = pl.pallas_call(
        stats_kernel,
        out_shape=(f32(channels // ROWS, ROWS), f32(1, ROWS)),
        compiler_params=PARAMS,
    )(results)
    total = jnp.sum(over_channels(total))
    grad_rms = jnp.sqrt(total / (channels * lax.axis_size("ch") * (LENGTH + 1)))
    bf16 = jax.ShapeDtypeStruct((rows, channels), jnp.bfloat16)
    output, query_grad, key_grad, value_grad, filter_grad = pl.pallas_call(
        post_kernel,
        out_shape=(bf16, bf16, bf16, bf16, f32(rows, channels)),
        compiler_params=PARAMS,
        cost_estimate=pl.CostEstimate(flops=10**6, bytes_accessed=2 * 10**6, transcendentals=0),
    )(results, query, key, value, cotangent, gain[None, :])
    return (
        output,
        query_grad,
        key_grad,
        value_grad,
        filter_grad,
        skip_grad.reshape(channels),
        grad_rms,
    )


def solution(mesh):
    both = P("seq", "ch")
    return jax.shard_map(
        body,
        mesh=mesh,
        in_specs=(both, both, both, both, both, P("ch")),
        out_specs=(both, both, both, both, both, P("ch"), P()),
        check_vma=False,
    )
```

```python
import functools
import math

import jax
import jax.numpy as jnp
import numpy as np
from jax import lax
from jax.experimental import pallas as pl
from jax.experimental.pallas import tpu as pltpu
from jax.sharding import PartitionSpec as P

ROWS = 128
BLOCKS = 32
LENGTH = ROWS * BLOCKS
CH_EACH = 16
LINES = 3 * CH_EACH
GROUP = 8
BACK = LINES + 1
ORDER = list(range(BLOCKS))
PLACE = [ORDER.index(s) for s in range(BLOCKS)]


def tables():
    n2 = np.arange(ROWS)
    k1 = np.arange(BLOCKS)
    angle = 2.0 * np.pi * n2[None, :] * (k1[:, None] + 0.25) / LENGTH
    twiddle = np.stack([np.cos(angle), -np.sin(angle)]).astype(np.float32)
    angle = 2.0 * np.pi * ((n2[:, None] * n2[None, :]) % ROWS) / ROWS
    cosine, sine = np.cos(angle), np.sin(angle)
    whole = np.block([[cosine, -sine], [sine, cosine]]).astype(np.float32)
    high = whole.astype(jnp.bfloat16)
    low = (whole - high.astype(np.float32)).astype(jnp.bfloat16)
    return twiddle, np.stack([high, low])


def times(value, angle):
    re, im = value
    turn = round(angle / (math.pi / 4), 9) % 8
    half = math.sqrt(0.5)
    if turn == 0:
        return re, im
    if turn == 2:
        return im, -re
    if turn == 1:
        return (re + im) * half, (im - re) * half
    if turn == 3:
        return (im - re) * half, -(re + im) * half
    c, s = math.cos(angle), math.sin(angle)
    return re * c + im * s, im * c - re * s


def add(a, b):
    return a[0] + b[0], a[1] + b[1]


def sub(a, b):
    return a[0] - b[0], a[1] - b[1]


def split_radix(values):
    count = len(values)
    if count == 1:
        return values
    if count == 2:
        return [add(*values), sub(*values)]
    even = split_radix(values[0::2])
    first = split_radix(values[1::4])
    third = split_radix(values[3::4])
    quarter = count // 4
    out = [None] * count
    for k in range(quarter):
        one = times(first[k], 2 * math.pi * k / count)
        two = times(third[k], 2 * math.pi * 3 * k / count)
        total, diff = add(one, two), sub(one, two)
        out[k] = add(even[k], total)
        out[k + 2 * quarter] = sub(even[k], total)
        e_re, e_im = even[k + quarter]
        out[k + quarter] = (e_re + diff[1], e_im - diff[0])
        out[k + 3 * quarter] = (e_re - diff[1], e_im + diff[0])
    return out


def pre_kernel(q_hbm, k_hbm, v_hbm, cot_hbm, taps_hbm, out_hbm, *scratch):
    buffers, out_ref, in_sems, out_sems = scratch[:5], *scratch[5:]
    sources = (q_hbm, k_hbm, v_hbm, cot_hbm, taps_hbm)
    loads = [pltpu.make_async_copy(sources[i], buffers[i], in_sems.at[i]) for i in range(5)]
    for i in (4, 1, 2, 0, 3):
        loads[i].start()
    stores = []
    for index, needs in ((2, (4,)), (0, (1, 2)), (1, (0, 3))):
        signal = None
        for i in needs:
            loads[i].wait()
            factor = buffers[i][...].astype(jnp.float32)
            signal = factor if signal is None else signal * factor
        lines = signal.T.reshape(BLOCKS, CH_EACH, ROWS)
        for s in range(BLOCKS):
            out_ref[index, PLACE[s]] = lines[s]
        here = slice(index * CH_EACH, (index + 1) * CH_EACH)
        store = pltpu.make_async_copy(
            out_ref.at[index], out_hbm.at[:, here, :], out_sems.at[index]
        )
        store.start()
        stores.append(store)
    for store in stores:
        store.wait()


def split(value):
    high = value.astype(jnp.bfloat16)
    low = (value - high.astype(jnp.float32)).astype(jnp.bfloat16)
    return high, low


def dft_rows(value, mat_ref):
    high, low = split(value)

    def dot(left, right):
        return jnp.dot(left, right, preferred_element_type=jnp.float32)

    return dot(high, mat_ref[0]) + (dot(low, mat_ref[0]) + dot(high, mat_ref[1]))


def coarse(in_ref, tw_ref, mid_ref, source, target):
    values = []
    for s in range(BLOCKS):
        signal = in_ref[PLACE[s], source, :]
        angle = 2 * math.pi * s / (4 * BLOCKS)
        values.append((signal * math.cos(angle), signal * -math.sin(angle)))
    for k1, (re, im) in enumerate(split_radix(values)):
        t_re, t_im = tw_ref[0, k1 : k1 + 1, :], tw_ref[1, k1 : k1 + 1, :]
        mid_ref[k1, target, :ROWS] = re * t_re - im * t_im
        mid_ref[k1, target, ROWS:] = re * t_im + im * t_re


def coarse_back(mid_ref, lines, scale):
    values = [(mid_ref[k1, lines, :ROWS], mid_ref[k1, lines, ROWS:]) for k1 in range(BLOCKS)]
    for s, (re, im) in enumerate(split_radix(values)):
        angle = 2 * math.pi * s / (4 * BLOCKS)
        yield s, re * (math.cos(angle) * scale) + im * (math.sin(angle) * scale)


def fine(value, mat_ref):
    groups, lines, width = value.shape
    return dft_rows(value.reshape(groups * lines, width), mat_ref).reshape(groups, lines, width)


def halves(value):
    return value[:, :, :ROWS], value[:, :, ROWS:]


def conj_times(a, b):
    (a_re, a_im), (b_re, b_im) = a, b
    return jnp.concatenate([a_re * b_re - a_im * b_im, -(a_re * b_im + a_im * b_re)], axis=2)


def conj_corr(a, b):
    (a_re, a_im), (b_re, b_im) = a, b
    return jnp.concatenate([a_re * b_re + a_im * b_im, a_re * b_im - a_im * b_re], axis=2)


def turned(value, tw_ref, here):
    re, im = halves(value)
    t_re, t_im = tw_ref[0, here, :][:, None, :], tw_ref[1, here, :][:, None, :]
    return re * t_re - im * t_im, re * t_im + im * t_re


def eight(step):
    return pl.ds(pl.multiple_of(step * 8, 8), 8)


def grad_kernel(in_ref, tw_ref, mat_ref, grad_ref, spec_ref, skip_ref, sq_ref, mid_ref, back_ref):
    @pl.loop(0, 2 * CH_EACH // 8)
    def _(step):
        coarse(in_ref, tw_ref, mid_ref, eight(step), eight(step))

    @pl.loop(0, BLOCKS // GROUP)
    def _(step):
        here = pl.ds(pl.multiple_of(step * GROUP, GROUP), GROUP)
        spectrum = fine(mid_ref[here], mat_ref)
        spec_ref[here] = spectrum
        mixed, gated = halves(spectrum[:, :CH_EACH]), halves(spectrum[:, CH_EACH:])
        re, im = turned(fine(conj_corr(gated, mixed), mat_ref), tw_ref, here)
        back_ref[here, :, :ROWS] = re
        back_ref[here, :, ROWS:] = im

    time_scale = 1.0 / math.sqrt(LENGTH)
    squares = jnp.zeros((8, ROWS), jnp.float32)
    for half in range(CH_EACH // 8):
        lines = slice(half * 8, half * 8 + 8)
        for s, series in coarse_back(back_ref, lines, time_scale / LENGTH):
            grad_ref[s, lines, :] = series
            squares = squares + series * series

    direct = jnp.zeros((CH_EACH, ROWS), jnp.float32)
    for s in range(BLOCKS):
        direct = direct + in_ref[s, :CH_EACH, :] * in_ref[s, CH_EACH : 2 * CH_EACH, :]
    direct = jnp.sum(direct, axis=1, keepdims=True) * time_scale
    row = lax.broadcasted_iota(jnp.int32, (CH_EACH, ROWS), 0)
    lane = lax.broadcasted_iota(jnp.int32, (CH_EACH, ROWS), 1)
    skip = jnp.sum(jnp.where(row == lane, direct, 0.0), axis=0, keepdims=True)
    skip_ref[...] = skip
    sq_ref[...] = jnp.sum(squares, axis=0, keepdims=True) + skip * skip


def taps_kernel(in_ref, tw_ref, mat_ref, gain_ref, spec_ref, gain_out_ref, mid_ref):
    gain_out_ref[...] = gain_ref[...]

    @pl.loop(0, CH_EACH // 8)
    def _(step):
        source = pl.ds(pl.multiple_of(step * 8 + 2 * CH_EACH, 8), 8)
        coarse(in_ref, tw_ref, mid_ref, source, eight(step))

    @pl.loop(0, BLOCKS // GROUP)
    def _(step):
        here = pl.ds(pl.multiple_of(step * GROUP, GROUP), GROUP)
        spec_ref[here] = fine(mid_ref[here], mat_ref)


def conv_kernel(spec_ref, taps_ref, tw_ref, mat_ref, grad_ref, out_ref, mid_ref):
    @pl.loop(0, BLOCKS // GROUP)
    def _(step):
        here = pl.ds(pl.multiple_of(step * GROUP, GROUP), GROUP)
        mixed, gated = halves(spec_ref[here, :CH_EACH]), halves(spec_ref[here, CH_EACH:])
        taps = halves(taps_ref[here])
        product = jnp.concatenate([conj_times(mixed, taps), conj_corr(gated, taps)], axis=1)
        re, im = turned(fine(product, mat_ref), tw_ref, here)
        mid_ref[here, :, :ROWS] = re
        mid_ref[here, :, ROWS:] = im

    for line in range(0, 2 * CH_EACH, 8):
        for s, series in coarse_back(mid_ref, slice(line, line + 8), 1.0 / LENGTH):
            first = PLACE[s] * BACK + line
            out_ref[first : first + 8, :] = series
    for s in range(BLOCKS):
        first = PLACE[s] * BACK + 2 * CH_EACH
        out_ref[first : first + CH_EACH, :] = grad_ref[s]
        out_ref[first + CH_EACH : first + CH_EACH + 1, :] = jnp.zeros((1, ROWS), jnp.float32)


def last_line_kernel(held_ref, skip_ref, *refs):
    one, two, four, six, out_ref = refs
    squares = (one[...] + two[...]) + (four[...] + six[...])
    squares = jnp.sum(squares, axis=1, keepdims=True)
    lane = lax.broadcasted_iota(jnp.int32, (1, ROWS), 1)
    line = jnp.where(lane == CH_EACH, squares, skip_ref[...])
    out_ref[...] = held_ref[...]
    for s in range(BLOCKS):
        out_ref[s * BACK + LINES : (s + 1) * BACK, :] = line


def statistics(in_ref, skip_ref, rms_ref, count):
    per_row = ROWS // CH_EACH
    rows = BLOCKS // per_row
    lane = lax.broadcasted_iota(jnp.int32, (rows, ROWS), 1)
    skip = jnp.zeros((rows, ROWS), jnp.float32)
    squares = jnp.zeros((rows, ROWS), jnp.float32)
    for m in range(per_row):
        at = [PLACE[r * per_row + m] * BACK + LINES for r in range(rows)]
        lines = jnp.concatenate([in_ref[i : i + 1, :] for i in at], axis=0)
        squares = squares + jnp.where(lane == CH_EACH, lines, 0.0)
        moved = pltpu.roll(lines, m * CH_EACH, 1) if m else lines
        skip = jnp.where(lane // CH_EACH == m, moved, skip)
    skip_ref[...] = skip
    total = jnp.sum(jnp.sum(squares, axis=0, keepdims=True), axis=1, keepdims=True)
    rms_ref[...] = jnp.sqrt(total * (1.0 / count))


def post_kernel(count, in_ref, q_ref, k_ref, v_ref, cot_ref, gain_ref, *outs):
    out_ref, dq_ref, dk_ref, dv_ref, dh_ref, skip_ref, rms_ref = outs
    statistics(in_ref, skip_ref, rms_ref, count)

    def series(index):
        first = [PLACE[s] * BACK + index * CH_EACH for s in range(BLOCKS)]
        return jnp.concatenate([in_ref[i : i + CH_EACH, :] for i in first], axis=0).T

    query = q_ref[...].astype(jnp.float32)
    key = k_ref[...].astype(jnp.float32)
    value = v_ref[...].astype(jnp.float32)
    cot = cot_ref[...].astype(jnp.float32)
    gain = gain_ref[...]
    inner = series(0) + gain * (key * value)
    out_ref[...] = (query * inner).astype(jnp.bfloat16)
    dq_ref[...] = (cot * inner).astype(jnp.bfloat16)
    mixed_grad = series(1) + gain * (query * cot)
    dk_ref[...] = (mixed_grad * value).astype(jnp.bfloat16)
    dv_ref[...] = (mixed_grad * key).astype(jnp.bfloat16)
    dh_ref[...] = series(2)


def partner(array, bit):
    return lax.ppermute(array, "ch", [(i, i ^ bit) for i in range(lax.axis_size("ch"))])


def exchange(array):
    return lax.all_to_all(array, "seq", 0, 0, axis_index_groups=[ORDER], tiled=True)


def f32(*shape):
    return jax.ShapeDtypeStruct(shape, jnp.float32)


PARAMS = pltpu.CompilerParams(vmem_limit_bytes=40 * 2**20)
COST = pl.CostEstimate(flops=2 * 10**9, bytes_accessed=4 * 10**6, transcendentals=0)
WIDE = pltpu.CompilerParams(vmem_limit_bytes=60 * 2**20)


def body(query, key, value, cotangent, taps, gain):
    rows, channels = query.shape
    twiddle, matrix = tables()
    signals = (query, key, value, cotangent, taps)
    hbm = pl.BlockSpec(memory_space=pltpu.HBM)
    packed = pl.pallas_call(
        pre_kernel,
        out_shape=f32(BLOCKS, LINES, ROWS),
        in_specs=[hbm] * len(signals),
        out_specs=hbm,
        scratch_shapes=[pltpu.VMEM(signal.shape, signal.dtype) for signal in signals]
        + [
            pltpu.VMEM((3, BLOCKS, CH_EACH, ROWS), jnp.float32),
            pltpu.SemaphoreType.DMA((len(signals),)),
            pltpu.SemaphoreType.DMA((3,)),
        ],
        compiler_params=WIDE,
    )(*signals)
    lines = exchange(packed)
    room = functools.partial(pltpu.VMEM, dtype=jnp.float32)
    grad, spectra, skip_part, squares = pl.pallas_call(
        grad_kernel,
        out_shape=(
            f32(BLOCKS, CH_EACH, ROWS),
            f32(BLOCKS, 2 * CH_EACH, 2 * ROWS),
            f32(1, ROWS),
            f32(1, ROWS),
        ),
        scratch_shapes=[
            room((BLOCKS, 2 * CH_EACH, 2 * ROWS)),
            room((BLOCKS, CH_EACH, 2 * ROWS)),
        ],
        compiler_params=PARAMS,
        cost_estimate=COST,
    )(lines, twiddle, matrix)
    squares = squares + partner(squares, 1)
    taps_spectrum, gain = pl.pallas_call(
        taps_kernel,
        out_shape=(f32(BLOCKS, CH_EACH, 2 * ROWS), f32(1, channels)),
        scratch_shapes=[room((BLOCKS, CH_EACH, 2 * ROWS))],
        compiler_params=PARAMS,
        cost_estimate=COST,
    )(lines, twiddle, matrix, gain[None, :])
    shares = [squares] + [partner(squares, bit) for bit in (2, 4, 6)]
    returned = pl.pallas_call(
        conv_kernel,
        out_shape=f32(BLOCKS * BACK, ROWS),
        scratch_shapes=[room((BLOCKS, 2 * CH_EACH, 2 * ROWS))],
        compiler_params=PARAMS,
        cost_estimate=COST,
    )(spectra, taps_spectrum, twiddle, matrix, grad)
    returned = pl.pallas_call(
        last_line_kernel,
        out_shape=f32(BLOCKS * BACK, ROWS),
        compiler_params=PARAMS,
    )(returned, skip_part, *shares)
    returned = exchange(returned.reshape(BLOCKS, BACK, 1, ROWS)).reshape(BLOCKS * BACK, ROWS)
    bf16 = jax.ShapeDtypeStruct((rows, channels), jnp.bfloat16)
    count = channels * lax.axis_size("ch") * (LENGTH + 1)
    *outputs, skip_grad, grad_rms = pl.pallas_call(
        functools.partial(post_kernel, count),
        out_shape=(
            *[bf16] * 4,
            f32(rows, channels),
            f32(channels // ROWS, ROWS),
            f32(1, 1),
        ),
        compiler_params=PARAMS,
    )(returned, query, key, value, cotangent, gain)
    return (*outputs, skip_grad.reshape(channels), grad_rms[0, 0])


def solution(mesh):
    both = P("seq", "ch")
    return jax.shard_map(
        body,
        mesh=mesh,
        in_specs=(both, both, both, both, both, P("ch")),
        out_specs=(both, both, both, both, both, P("ch"), P()),
        check_vma=False,
    )
```

```python
import functools
import math

import jax
import jax.numpy as jnp
import numpy as np
from jax import lax
from jax.experimental import pallas as pl
from jax.experimental.pallas import tpu as pltpu
from jax.sharding import PartitionSpec as P

ROWS = 128
BLOCKS = 32
LENGTH = ROWS * BLOCKS
CH_EACH = 16
LINES = 3 * CH_EACH
GROUP = 32
WIDER = 32
BACK = LINES + 1
ORDER = [12, 30, 2, 15, 20, 25, 27, 28, 0, 6, 5, 18, 19, 9, 29, 7, 26, 22, 14, 31, 8, 23, 21, 1, 16, 17, 24, 10, 3, 13, 11, 4]
PLACE = [ORDER.index(s) for s in range(BLOCKS)]


def tables():
    n2 = np.arange(ROWS)
    k1 = np.arange(BLOCKS)
    angle = 2.0 * np.pi * n2[None, :] * (k1[:, None] + 0.25) / LENGTH
    twiddle = np.stack([np.cos(angle), -np.sin(angle)]).astype(np.float32)
    angle = 2.0 * np.pi * ((n2[:, None] * n2[None, :]) % ROWS) / ROWS
    cosine, sine = np.cos(angle), np.sin(angle)
    whole = np.block([[cosine, -sine], [sine, cosine]]).astype(np.float32)
    high = whole.astype(jnp.bfloat16)
    low = (whole - high.astype(np.float32)).astype(jnp.bfloat16)
    return twiddle, np.stack([high, low])


def times(value, angle):
    re, im = value
    turn = round(angle / (math.pi / 4), 9) % 8
    half = math.sqrt(0.5)
    if turn == 0:
        return re, im
    if turn == 2:
        return im, -re
    if turn == 1:
        return (re + im) * half, (im - re) * half
    if turn == 3:
        return (im - re) * half, -(re + im) * half
    c, s = math.cos(angle), math.sin(angle)
    return re * c + im * s, im * c - re * s


def add(a, b):
    return a[0] + b[0], a[1] + b[1]


def sub(a, b):
    return a[0] - b[0], a[1] - b[1]


def split_radix(values):
    count = len(values)
    if count == 1:
        return values
    if count == 2:
        return [add(*values), sub(*values)]
    even = split_radix(values[0::2])
    first = split_radix(values[1::4])
    third = split_radix(values[3::4])
    quarter = count // 4
    out = [None] * count
    for k in range(quarter):
        one = times(first[k], 2 * math.pi * k / count)
        two = times(third[k], 2 * math.pi * 3 * k / count)
        total, diff = add(one, two), sub(one, two)
        out[k] = add(even[k], total)
        out[k + 2 * quarter] = sub(even[k], total)
        e_re, e_im = even[k + quarter]
        out[k + quarter] = (e_re + diff[1], e_im - diff[0])
        out[k + 3 * quarter] = (e_re - diff[1], e_im + diff[0])
    return out


def pre_kernel(q_hbm, k_hbm, v_hbm, cot_hbm, taps_hbm, out_hbm, *scratch):
    buffers, out_ref, in_sems, out_sems = scratch[:5], *scratch[5:]
    sources = (q_hbm, k_hbm, v_hbm, cot_hbm, taps_hbm)
    loads = [pltpu.make_async_copy(sources[i], buffers[i], in_sems.at[i]) for i in range(5)]
    for i in (4, 1, 2, 0, 3):
        loads[i].start()
    stores = []
    for index, needs in ((2, (4,)), (0, (1, 2)), (1, (0, 3))):
        signal = None
        for i in needs:
            loads[i].wait()
            factor = buffers[i][...].astype(jnp.float32)
            signal = factor if signal is None else signal * factor
        lines = signal.T.reshape(BLOCKS, CH_EACH, ROWS)
        for s in range(BLOCKS):
            out_ref[index, PLACE[s]] = lines[s]
        here = slice(index * CH_EACH, (index + 1) * CH_EACH)
        store = pltpu.make_async_copy(
            out_ref.at[index], out_hbm.at[:, here, :], out_sems.at[index]
        )
        store.start()
        stores.append(store)
    for store in stores:
        store.wait()


def split(value):
    high = value.astype(jnp.bfloat16)
    low = (value - high.astype(jnp.float32)).astype(jnp.bfloat16)
    return high, low


def dft_rows(value, mat_ref):
    high, low = split(value)

    def dot(left, right):
        return jnp.dot(left, right, preferred_element_type=jnp.float32)

    return dot(high, mat_ref[0]) + (dot(low, mat_ref[0]) + dot(high, mat_ref[1]))


def coarse(in_ref, tw_ref, mid_ref, source, target):
    values = []
    for s in range(BLOCKS):
        signal = in_ref[PLACE[s], source, :]
        angle = 2 * math.pi * s / (4 * BLOCKS)
        values.append((signal * math.cos(angle), signal * -math.sin(angle)))
    for k1, (re, im) in enumerate(split_radix(values)):
        t_re, t_im = tw_ref[0, k1 : k1 + 1, :], tw_ref[1, k1 : k1 + 1, :]
        mid_ref[k1, target, :ROWS] = re * t_re - im * t_im
        mid_ref[k1, target, ROWS:] = re * t_im + im * t_re


def coarse_back(mid_ref, lines, scale):
    values = [(mid_ref[k1, lines, :ROWS], mid_ref[k1, lines, ROWS:]) for k1 in range(BLOCKS)]
    for s, (re, im) in enumerate(split_radix(values)):
        angle = 2 * math.pi * s / (4 * BLOCKS)
        yield s, re * (math.cos(angle) * scale) + im * (math.sin(angle) * scale)


def fine(value, mat_ref):
    groups, lines, width = value.shape
    return dft_rows(value.reshape(groups * lines, width), mat_ref).reshape(groups, lines, width)


def halves(value):
    return value[:, :, :ROWS], value[:, :, ROWS:]


def conj_times(a, b):
    (a_re, a_im), (b_re, b_im) = a, b
    return jnp.concatenate([a_re * b_re - a_im * b_im, -(a_re * b_im + a_im * b_re)], axis=2)


def conj_corr(a, b):
    (a_re, a_im), (b_re, b_im) = a, b
    return jnp.concatenate([a_re * b_re + a_im * b_im, a_re * b_im - a_im * b_re], axis=2)


def turned(value, tw_ref, here):
    re, im = halves(value)
    t_re, t_im = tw_ref[0, here, :][:, None, :], tw_ref[1, here, :][:, None, :]
    return re * t_re - im * t_im, re * t_im + im * t_re


def eight(step):
    return pl.ds(pl.multiple_of(step * 8, 8), 8)


def grad_kernel(in_ref, tw_ref, mat_ref, gain_ref, *refs):
    grad_ref, spec_ref, skip_ref, sq_ref, gain_out_ref, mid_ref, back_ref = refs
    gain_out_ref[...] = gain_ref[...]

    @pl.loop(0, 2 * CH_EACH // 8)
    def _(step):
        coarse(in_ref, tw_ref, mid_ref, eight(step), eight(step))

    @pl.loop(0, BLOCKS // GROUP)
    def _(step):
        here = pl.ds(pl.multiple_of(step * GROUP, GROUP), GROUP)
        spectrum = fine(mid_ref[here], mat_ref)
        spec_ref[here] = spectrum
        mixed, gated = halves(spectrum[:, :CH_EACH]), halves(spectrum[:, CH_EACH:])
        re, im = turned(fine(conj_corr(gated, mixed), mat_ref), tw_ref, here)
        back_ref[here, :, :ROWS] = re
        back_ref[here, :, ROWS:] = im

    time_scale = 1.0 / math.sqrt(LENGTH)
    squares = jnp.zeros((8, ROWS), jnp.float32)
    for half in range(CH_EACH // 8):
        lines = slice(half * 8, half * 8 + 8)
        for s, series in coarse_back(back_ref, lines, time_scale / LENGTH):
            grad_ref[s, lines, :] = series
            squares = squares + series * series

    direct = jnp.zeros((CH_EACH, ROWS), jnp.float32)
    for s in range(BLOCKS):
        direct = direct + in_ref[s, :CH_EACH, :] * in_ref[s, CH_EACH : 2 * CH_EACH, :]
    direct = jnp.sum(direct, axis=1, keepdims=True) * time_scale
    row = lax.broadcasted_iota(jnp.int32, (CH_EACH, ROWS), 0)
    lane = lax.broadcasted_iota(jnp.int32, (CH_EACH, ROWS), 1)
    skip = jnp.sum(jnp.where(row == lane, direct, 0.0), axis=0, keepdims=True)
    skip_ref[...] = skip
    sq_ref[...] = jnp.sum(squares, axis=0, keepdims=True) + skip * skip


def taps_kernel(in_ref, tw_ref, mat_ref, spec_ref, mid_ref):
    @pl.loop(0, CH_EACH // 8)
    def _(step):
        source = pl.ds(pl.multiple_of(step * 8 + 2 * CH_EACH, 8), 8)
        coarse(in_ref, tw_ref, mid_ref, source, eight(step))

    @pl.loop(0, BLOCKS // WIDER)
    def _(step):
        here = pl.ds(pl.multiple_of(step * WIDER, WIDER), WIDER)
        spec_ref[here] = fine(mid_ref[here], mat_ref)


def conv_kernel(line, combine, spec_ref, taps_ref, tw_ref, mat_ref, after_ref, out_ref, mid_ref):
    @pl.loop(0, BLOCKS // WIDER)
    def _(step):
        here = pl.ds(pl.multiple_of(step * WIDER, WIDER), WIDER)
        signal = halves(spec_ref[here, line : line + CH_EACH])
        product = combine(signal, halves(taps_ref[here]))
        re, im = turned(fine(product, mat_ref), tw_ref, here)
        mid_ref[here, :, :ROWS] = re
        mid_ref[here, :, ROWS:] = im

    for first in range(0, CH_EACH, 8):
        lines = slice(first, first + 8)
        for s, series in coarse_back(mid_ref, lines, 1.0 / LENGTH):
            out_ref[s, lines, :] = series


def pack_kernel(conv_ref, back_ref, grad_ref, skip_ref, one_ref, two_ref, out_ref):
    squares = jnp.sum(one_ref[...] + two_ref[...], axis=1, keepdims=True)
    lane = lax.broadcasted_iota(jnp.int32, (1, ROWS), 1)
    last = jnp.where(lane == CH_EACH, squares, skip_ref[...])
    for s in range(BLOCKS):
        first = PLACE[s] * BACK
        for ref in (conv_ref, back_ref, grad_ref):
            out_ref[first : first + CH_EACH, :] = ref[s]
            first += CH_EACH
        out_ref[first : first + 1, :] = last


def statistics(in_ref, skip_ref, rms_ref, count):
    per_row = ROWS // CH_EACH
    rows = BLOCKS // per_row
    lane = lax.broadcasted_iota(jnp.int32, (rows, ROWS), 1)
    skip = jnp.zeros((rows, ROWS), jnp.float32)
    squares = jnp.zeros((rows, ROWS), jnp.float32)
    for m in range(per_row):
        at = [PLACE[r * per_row + m] * BACK + LINES for r in range(rows)]
        lines = jnp.concatenate([in_ref[i : i + 1, :] for i in at], axis=0)
        squares = squares + jnp.where(lane == CH_EACH, lines, 0.0)
        moved = pltpu.roll(lines, m * CH_EACH, 1) if m else lines
        skip = jnp.where(lane // CH_EACH == m, moved, skip)
    skip_ref[...] = skip
    total = jnp.sum(jnp.sum(squares, axis=0, keepdims=True), axis=1, keepdims=True)
    rms_ref[...] = jnp.sqrt(total * (1.0 / count))


def post_kernel(count, in_ref, q_ref, k_ref, v_ref, cot_ref, gain_ref, *outs):
    out_ref, dq_ref, dk_ref, dv_ref, dh_ref, skip_ref, rms_ref = outs
    statistics(in_ref, skip_ref, rms_ref, count)

    def series(index):
        first = [PLACE[s] * BACK + index * CH_EACH for s in range(BLOCKS)]
        return jnp.concatenate([in_ref[i : i + CH_EACH, :] for i in first], axis=0).T

    query = q_ref[...].astype(jnp.float32)
    key = k_ref[...].astype(jnp.float32)
    value = v_ref[...].astype(jnp.float32)
    cot = cot_ref[...].astype(jnp.float32)
    gain = gain_ref[...]
    inner = series(0) + gain * (key * value)
    out_ref[...] = (query * inner).astype(jnp.bfloat16)
    dq_ref[...] = (cot * inner).astype(jnp.bfloat16)
    mixed_grad = series(1) + gain * (query * cot)
    dk_ref[...] = (mixed_grad * value).astype(jnp.bfloat16)
    dv_ref[...] = (mixed_grad * key).astype(jnp.bfloat16)
    dh_ref[...] = series(2)


def partner(array, bit):
    return lax.ppermute(array, "ch", [(i, i ^ bit) for i in range(lax.axis_size("ch"))])


def exchange(array):
    return lax.all_to_all(array, "seq", 0, 0, axis_index_groups=[ORDER], tiled=True)


def f32(*shape):
    return jax.ShapeDtypeStruct(shape, jnp.float32)


PARAMS = pltpu.CompilerParams(vmem_limit_bytes=40 * 2**20)
COST = pl.CostEstimate(flops=2 * 10**9, bytes_accessed=4 * 10**6, transcendentals=0)
WIDE = pltpu.CompilerParams(vmem_limit_bytes=60 * 2**20)


def body(query, key, value, cotangent, taps, gain):
    rows, channels = query.shape
    twiddle, matrix = tables()
    signals = (query, key, value, cotangent, taps)
    hbm = pl.BlockSpec(memory_space=pltpu.HBM)
    packed = pl.pallas_call(
        pre_kernel,
        out_shape=f32(BLOCKS, LINES, ROWS),
        in_specs=[hbm] * len(signals),
        out_specs=hbm,
        scratch_shapes=[pltpu.VMEM(signal.shape, signal.dtype) for signal in signals]
        + [
            pltpu.VMEM((3, BLOCKS, CH_EACH, ROWS), jnp.float32),
            pltpu.SemaphoreType.DMA((len(signals),)),
            pltpu.SemaphoreType.DMA((3,)),
        ],
        compiler_params=WIDE,
    )(*signals)
    lines = exchange(packed)
    room = functools.partial(pltpu.VMEM, dtype=jnp.float32)
    grad, spectra, skip_part, squares, gain = pl.pallas_call(
        grad_kernel,
        out_shape=(
            f32(BLOCKS, CH_EACH, ROWS),
            f32(BLOCKS, 2 * CH_EACH, 2 * ROWS),
            f32(1, ROWS),
            f32(1, ROWS),
            f32(1, channels),
        ),
        scratch_shapes=[
            room((BLOCKS, 2 * CH_EACH, 2 * ROWS)),
            room((BLOCKS, CH_EACH, 2 * ROWS)),
        ],
        compiler_params=PARAMS,
        cost_estimate=COST,
    )(lines, twiddle, matrix, gain[None, :])
    squares = squares + partner(squares, 1)
    taps_spectrum = pl.pallas_call(
        taps_kernel,
        out_shape=f32(BLOCKS, CH_EACH, 2 * ROWS),
        scratch_shapes=[room((BLOCKS, CH_EACH, 2 * ROWS))],
        compiler_params=PARAMS,
        cost_estimate=COST,
    )(lines, twiddle, matrix)

    def convolution(line, combine, after):
        return pl.pallas_call(
            functools.partial(conv_kernel, line, combine),
            out_shape=f32(BLOCKS, CH_EACH, ROWS),
            scratch_shapes=[room((BLOCKS, CH_EACH, 2 * ROWS))],
            compiler_params=PARAMS,
            cost_estimate=COST,
        )(spectra, taps_spectrum, twiddle, matrix, after)

    conv = convolution(0, conj_times, squares)
    squares = squares + partner(squares, 2)
    back = convolution(CH_EACH, conj_corr, squares)
    returned = pl.pallas_call(
        pack_kernel,
        out_shape=f32(BLOCKS * BACK, ROWS),
        compiler_params=PARAMS,
    )(conv, back, grad, skip_part, squares, partner(squares, 6))
    returned = exchange(returned.reshape(BLOCKS, BACK, 1, ROWS)).reshape(BLOCKS * BACK, ROWS)
    bf16 = jax.ShapeDtypeStruct((rows, channels), jnp.bfloat16)
    count = channels * lax.axis_size("ch") * (LENGTH + 1)
    *outputs, skip_grad, grad_rms = pl.pallas_call(
        functools.partial(post_kernel, count),
        out_shape=(
            *[bf16] * 4,
            f32(rows, channels),
            f32(channels // ROWS, ROWS),
            f32(1, 1),
        ),
        compiler_params=PARAMS,
    )(returned, query, key, value, cotangent, gain)
    return (*outputs, skip_grad.reshape(channels), grad_rms[0, 0])


def solution(mesh):
    both = P("seq", "ch")
    return jax.shard_map(
        body,
        mesh=mesh,
        in_specs=(both, both, both, both, both, P("ch")),
        out_specs=(both, both, both, both, both, P("ch"), P()),
        check_vma=False,
    )
```

```python
import functools
import math

import jax
import jax.numpy as jnp
import numpy as np
from jax import lax
from jax.experimental import pallas as pl
from jax.experimental.pallas import tpu as pltpu
from jax.sharding import PartitionSpec as P

ROWS = 128
BLOCKS = 32
LENGTH = ROWS * BLOCKS
CH_EACH = 16
LINES = 3 * CH_EACH
GROUP = 32
WIDER = 32
BACK = LINES + 1
ORDER = [
    23, 20, 27, 29, 10, 22, 12, 1, 0, 24, 28, 19, 6, 18, 21, 11,
    2, 31, 16, 26, 5, 15, 3, 17, 8, 30, 14, 25, 7, 13, 9, 4,
]
PLACE = [ORDER.index(s) for s in range(BLOCKS)]


def tables():
    n2 = np.arange(ROWS)
    k1 = np.arange(BLOCKS)
    angle = 2.0 * np.pi * n2[None, :] * (k1[:, None] + 0.25) / LENGTH
    twiddle = np.stack([np.cos(angle), -np.sin(angle)]).astype(np.float32)
    angle = 2.0 * np.pi * ((n2[:, None] * n2[None, :]) % ROWS) / ROWS
    cosine, sine = np.cos(angle), np.sin(angle)
    whole = np.block([[cosine, -sine], [sine, cosine]]).astype(np.float32)
    high = whole.astype(jnp.bfloat16)
    low = (whole - high.astype(np.float32)).astype(jnp.bfloat16)
    return twiddle, np.stack([high, low])


def times(value, angle):
    re, im = value
    turn = round(angle / (math.pi / 4), 9) % 8
    half = math.sqrt(0.5)
    if turn == 0:
        return re, im
    if turn == 2:
        return im, -re
    if turn == 1:
        return (re + im) * half, (im - re) * half
    if turn == 3:
        return (im - re) * half, -(re + im) * half
    c, s = math.cos(angle), math.sin(angle)
    return re * c + im * s, im * c - re * s


def add(a, b):
    return a[0] + b[0], a[1] + b[1]


def sub(a, b):
    return a[0] - b[0], a[1] - b[1]


def split_radix(values):
    count = len(values)
    if count == 1:
        return values
    if count == 2:
        return [add(*values), sub(*values)]
    even = split_radix(values[0::2])
    first = split_radix(values[1::4])
    third = split_radix(values[3::4])
    quarter = count // 4
    out = [None] * count
    for k in range(quarter):
        one = times(first[k], 2 * math.pi * k / count)
        two = times(third[k], 2 * math.pi * 3 * k / count)
        total, diff = add(one, two), sub(one, two)
        out[k] = add(even[k], total)
        out[k + 2 * quarter] = sub(even[k], total)
        e_re, e_im = even[k + quarter]
        out[k + quarter] = (e_re + diff[1], e_im - diff[0])
        out[k + 3 * quarter] = (e_re - diff[1], e_im + diff[0])
    return out


def pre_kernel(q_hbm, k_hbm, v_hbm, cot_hbm, taps_hbm, out_hbm, *scratch):
    buffers, out_ref, in_sems, out_sems = scratch[:5], *scratch[5:]
    sources = (q_hbm, k_hbm, v_hbm, cot_hbm, taps_hbm)
    loads = [pltpu.make_async_copy(sources[i], buffers[i], in_sems.at[i]) for i in range(5)]
    for i in (4, 1, 2, 0, 3):
        loads[i].start()
    stores = []
    for index, needs in ((2, (4,)), (0, (1, 2)), (1, (0, 3))):
        signal = None
        for i in needs:
            loads[i].wait()
            factor = buffers[i][...].astype(jnp.float32)
            signal = factor if signal is None else signal * factor
        lines = signal.T.reshape(BLOCKS, CH_EACH, ROWS)
        for s in range(BLOCKS):
            out_ref[index, PLACE[s]] = lines[s]
        here = slice(index * CH_EACH, (index + 1) * CH_EACH)
        store = pltpu.make_async_copy(
            out_ref.at[index], out_hbm.at[:, here, :], out_sems.at[index]
        )
        store.start()
        stores.append(store)
    for store in stores:
        store.wait()


def split(value):
    high = value.astype(jnp.bfloat16)
    low = (value - high.astype(jnp.float32)).astype(jnp.bfloat16)
    return high, low


def dft_rows(value, mat_ref):
    high, low = split(value)

    def dot(left, right):
        return jnp.dot(left, right, preferred_element_type=jnp.float32)

    return dot(high, mat_ref[0]) + (dot(low, mat_ref[0]) + dot(high, mat_ref[1]))


def coarse(in_ref, tw_ref, mid_ref, source, target):
    values = []
    for s in range(BLOCKS):
        signal = in_ref[PLACE[s], source, :]
        angle = 2 * math.pi * s / (4 * BLOCKS)
        values.append((signal * math.cos(angle), signal * -math.sin(angle)))
    for k1, (re, im) in enumerate(split_radix(values)):
        t_re, t_im = tw_ref[0, k1 : k1 + 1, :], tw_ref[1, k1 : k1 + 1, :]
        mid_ref[k1, target, :ROWS] = re * t_re - im * t_im
        mid_ref[k1, target, ROWS:] = re * t_im + im * t_re


def coarse_back(mid_ref, lines, scale):
    values = [(mid_ref[k1, lines, :ROWS], mid_ref[k1, lines, ROWS:]) for k1 in range(BLOCKS)]
    for s, (re, im) in enumerate(split_radix(values)):
        angle = 2 * math.pi * s / (4 * BLOCKS)
        yield s, re * (math.cos(angle) * scale) + im * (math.sin(angle) * scale)


def fine(value, mat_ref):
    groups, lines, width = value.shape
    return dft_rows(value.reshape(groups * lines, width), mat_ref).reshape(groups, lines, width)


def halves(value):
    return value[:, :, :ROWS], value[:, :, ROWS:]


def conj_times(a, b):
    (a_re, a_im), (b_re, b_im) = a, b
    return jnp.concatenate([a_re * b_re - a_im * b_im, -(a_re * b_im + a_im * b_re)], axis=2)


def conj_corr(a, b):
    (a_re, a_im), (b_re, b_im) = a, b
    return jnp.concatenate([a_re * b_re + a_im * b_im, a_re * b_im - a_im * b_re], axis=2)


def turned(value, tw_ref, here):
    re, im = halves(value)
    t_re, t_im = tw_ref[0, here, :][:, None, :], tw_ref[1, here, :][:, None, :]
    return re * t_re - im * t_im, re * t_im + im * t_re


def eight(step):
    return pl.ds(pl.multiple_of(step * 8, 8), 8)


def grad_kernel(in_ref, tw_ref, mat_ref, gain_ref, *refs):
    grad_ref, spec_ref, skip_ref, sq_ref, gain_out_ref, mid_ref, back_ref = refs
    gain_out_ref[...] = gain_ref[...]

    @pl.loop(0, 2 * CH_EACH // 8)
    def _(step):
        coarse(in_ref, tw_ref, mid_ref, eight(step), eight(step))

    @pl.loop(0, BLOCKS // GROUP)
    def _(step):
        here = pl.ds(pl.multiple_of(step * GROUP, GROUP), GROUP)
        spectrum = fine(mid_ref[here], mat_ref)
        spec_ref[here] = spectrum
        mixed, gated = halves(spectrum[:, :CH_EACH]), halves(spectrum[:, CH_EACH:])
        re, im = turned(fine(conj_corr(gated, mixed), mat_ref), tw_ref, here)
        back_ref[here, :, :ROWS] = re
        back_ref[here, :, ROWS:] = im

    time_scale = 1.0 / math.sqrt(LENGTH)
    squares = jnp.zeros((8, ROWS), jnp.float32)
    for half in range(CH_EACH // 8):
        lines = slice(half * 8, half * 8 + 8)
        for s, series in coarse_back(back_ref, lines, time_scale / LENGTH):
            grad_ref[s, lines, :] = series
            squares = squares + series * series

    direct = jnp.zeros((CH_EACH, ROWS), jnp.float32)
    for s in range(BLOCKS):
        direct = direct + in_ref[s, :CH_EACH, :] * in_ref[s, CH_EACH : 2 * CH_EACH, :]
    direct = jnp.sum(direct, axis=1, keepdims=True) * time_scale
    row = lax.broadcasted_iota(jnp.int32, (CH_EACH, ROWS), 0)
    lane = lax.broadcasted_iota(jnp.int32, (CH_EACH, ROWS), 1)
    skip = jnp.sum(jnp.where(row == lane, direct, 0.0), axis=0, keepdims=True)
    skip_ref[...] = skip
    sq_ref[...] = jnp.sum(squares, axis=0, keepdims=True) + skip * skip


def taps_kernel(in_ref, tw_ref, mat_ref, spec_ref, mid_ref):
    @pl.loop(0, CH_EACH // 8)
    def _(step):
        source = pl.ds(pl.multiple_of(step * 8 + 2 * CH_EACH, 8), 8)
        coarse(in_ref, tw_ref, mid_ref, source, eight(step))

    @pl.loop(0, BLOCKS // WIDER)
    def _(step):
        here = pl.ds(pl.multiple_of(step * WIDER, WIDER), WIDER)
        spec_ref[here] = fine(mid_ref[here], mat_ref)


def conv_kernel(line, combine, spec_ref, taps_ref, tw_ref, mat_ref, after_ref, out_ref, mid_ref):
    @pl.loop(0, BLOCKS // WIDER)
    def _(step):
        here = pl.ds(pl.multiple_of(step * WIDER, WIDER), WIDER)
        signal = halves(spec_ref[here, line : line + CH_EACH])
        product = combine(signal, halves(taps_ref[here]))
        re, im = turned(fine(product, mat_ref), tw_ref, here)
        mid_ref[here, :, :ROWS] = re
        mid_ref[here, :, ROWS:] = im

    for first in range(0, CH_EACH, 8):
        lines = slice(first, first + 8)
        for s, series in coarse_back(mid_ref, lines, 1.0 / LENGTH):
            out_ref[s, lines, :] = series


def pack_kernel(conv_ref, back_ref, grad_ref, skip_ref, *refs):
    own, two, four, six, out_ref = refs
    squares = (own[...] + two[...]) + (four[...] + six[...])
    squares = jnp.sum(squares, axis=1, keepdims=True)
    lane = lax.broadcasted_iota(jnp.int32, (1, ROWS), 1)
    last = jnp.where(lane == CH_EACH, squares, skip_ref[...])
    for s in range(BLOCKS):
        first = PLACE[s] * BACK
        for ref in (conv_ref, back_ref, grad_ref):
            out_ref[first : first + CH_EACH, :] = ref[s]
            first += CH_EACH
        out_ref[first : first + 1, :] = last


def statistics(in_ref, skip_ref, rms_ref, count):
    per_row = ROWS // CH_EACH
    rows = BLOCKS // per_row
    lane = lax.broadcasted_iota(jnp.int32, (rows, ROWS), 1)
    skip = jnp.zeros((rows, ROWS), jnp.float32)
    squares = jnp.zeros((rows, ROWS), jnp.float32)
    for m in range(per_row):
        at = [PLACE[r * per_row + m] * BACK + LINES for r in range(rows)]
        lines = jnp.concatenate([in_ref[i : i + 1, :] for i in at], axis=0)
        squares = squares + jnp.where(lane == CH_EACH, lines, 0.0)
        moved = pltpu.roll(lines, m * CH_EACH, 1) if m else lines
        skip = jnp.where(lane // CH_EACH == m, moved, skip)
    skip_ref[...] = skip
    total = jnp.sum(jnp.sum(squares, axis=0, keepdims=True), axis=1, keepdims=True)
    rms_ref[...] = jnp.sqrt(total * (1.0 / count))


def post_kernel(count, in_ref, q_ref, k_ref, v_ref, cot_ref, gain_ref, *outs):
    out_ref, dq_ref, dk_ref, dv_ref, dh_ref, skip_ref, rms_ref = outs
    statistics(in_ref, skip_ref, rms_ref, count)

    def series(index):
        first = [PLACE[s] * BACK + index * CH_EACH for s in range(BLOCKS)]
        return jnp.concatenate([in_ref[i : i + CH_EACH, :] for i in first], axis=0).T

    query = q_ref[...].astype(jnp.float32)
    key = k_ref[...].astype(jnp.float32)
    value = v_ref[...].astype(jnp.float32)
    cot = cot_ref[...].astype(jnp.float32)
    gain = gain_ref[...]
    inner = series(0) + gain * (key * value)
    out_ref[...] = (query * inner).astype(jnp.bfloat16)
    dq_ref[...] = (cot * inner).astype(jnp.bfloat16)
    mixed_grad = series(1) + gain * (query * cot)
    dk_ref[...] = (mixed_grad * value).astype(jnp.bfloat16)
    dv_ref[...] = (mixed_grad * key).astype(jnp.bfloat16)
    dh_ref[...] = series(2)


def partner(array, bit):
    return lax.ppermute(array, "ch", [(i, i ^ bit) for i in range(lax.axis_size("ch"))])


def exchange(array):
    return lax.all_to_all(array, "seq", 0, 0, axis_index_groups=[ORDER], tiled=True)


def f32(*shape):
    return jax.ShapeDtypeStruct(shape, jnp.float32)


PARAMS = pltpu.CompilerParams(vmem_limit_bytes=40 * 2**20)
COST = pl.CostEstimate(flops=2 * 10**9, bytes_accessed=4 * 10**6, transcendentals=0)
WIDE = pltpu.CompilerParams(vmem_limit_bytes=60 * 2**20)


def body(query, key, value, cotangent, taps, gain):
    rows, channels = query.shape
    twiddle, matrix = tables()
    signals = (query, key, value, cotangent, taps)
    hbm = pl.BlockSpec(memory_space=pltpu.HBM)
    packed = pl.pallas_call(
        pre_kernel,
        out_shape=f32(BLOCKS, LINES, ROWS),
        in_specs=[hbm] * len(signals),
        out_specs=hbm,
        scratch_shapes=[pltpu.VMEM(signal.shape, signal.dtype) for signal in signals]
        + [
            pltpu.VMEM((3, BLOCKS, CH_EACH, ROWS), jnp.float32),
            pltpu.SemaphoreType.DMA((len(signals),)),
            pltpu.SemaphoreType.DMA((3,)),
        ],
        compiler_params=WIDE,
    )(*signals)
    lines = exchange(packed)
    room = functools.partial(pltpu.VMEM, dtype=jnp.float32)
    grad, spectra, skip_part, squares, gain = pl.pallas_call(
        grad_kernel,
        out_shape=(
            f32(BLOCKS, CH_EACH, ROWS),
            f32(BLOCKS, 2 * CH_EACH, 2 * ROWS),
            f32(1, ROWS),
            f32(1, ROWS),
            f32(1, channels),
        ),
        scratch_shapes=[
            room((BLOCKS, 2 * CH_EACH, 2 * ROWS)),
            room((BLOCKS, CH_EACH, 2 * ROWS)),
        ],
        compiler_params=PARAMS,
        cost_estimate=COST,
    )(lines, twiddle, matrix, gain[None, :])
    squares = squares + partner(squares, 1)
    taps_spectrum = pl.pallas_call(
        taps_kernel,
        out_shape=f32(BLOCKS, CH_EACH, 2 * ROWS),
        scratch_shapes=[room((BLOCKS, CH_EACH, 2 * ROWS))],
        compiler_params=PARAMS,
        cost_estimate=COST,
    )(lines, twiddle, matrix)

    def convolution(line, combine, after):
        return pl.pallas_call(
            functools.partial(conv_kernel, line, combine),
            out_shape=f32(BLOCKS, CH_EACH, ROWS),
            scratch_shapes=[room((BLOCKS, CH_EACH, 2 * ROWS))],
            compiler_params=PARAMS,
            cost_estimate=COST,
        )(spectra, taps_spectrum, twiddle, matrix, after)

    conv = convolution(0, conj_times, squares)
    two, four, six = (partner(squares, bit) for bit in (2, 4, 6))
    back = convolution(CH_EACH, conj_corr, squares)
    returned = pl.pallas_call(
        pack_kernel,
        out_shape=f32(BLOCKS * BACK, ROWS),
        compiler_params=PARAMS,
    )(conv, back, grad, skip_part, squares, two, four, six)
    returned = exchange(returned.reshape(BLOCKS, BACK, 1, ROWS)).reshape(BLOCKS * BACK, ROWS)
    bf16 = jax.ShapeDtypeStruct((rows, channels), jnp.bfloat16)
    count = channels * lax.axis_size("ch") * (LENGTH + 1)
    *outputs, skip_grad, grad_rms = pl.pallas_call(
        functools.partial(post_kernel, count),
        out_shape=(
            *[bf16] * 4,
            f32(rows, channels),
            f32(channels // ROWS, ROWS),
            f32(1, 1),
        ),
        compiler_params=PARAMS,
    )(returned, query, key, value, cotangent, gain)
    return (*outputs, skip_grad.reshape(channels), grad_rms[0, 0])


def solution(mesh):
    both = P("seq", "ch")
    return jax.shard_map(
        body,
        mesh=mesh,
        in_specs=(both, both, both, both, both, P("ch")),
        out_specs=(both, both, both, both, both, P("ch"), P()),
        check_vma=False,
    )
```

```python
import functools
import math

import jax
import jax.numpy as jnp
import numpy as np
from jax import lax
from jax.experimental import pallas as pl
from jax.experimental.pallas import tpu as pltpu
from jax.sharding import PartitionSpec as P

ROWS = 128
BLOCKS = 32
LENGTH = ROWS * BLOCKS
CH_EACH = 16
LINES = 3 * CH_EACH
GROUP = 32
WIDER = 32
BACK = LINES + 1
ORDER = [
    23, 20, 27, 29, 10, 22, 12, 1, 0, 24, 28, 19, 6, 18, 21, 11,
    2, 31, 16, 26, 5, 15, 3, 17, 8, 30, 14, 25, 7, 13, 9, 4,
]
PLACE = [ORDER.index(s) for s in range(BLOCKS)]


def tables():
    n2 = np.arange(ROWS)
    k1 = np.arange(BLOCKS)
    angle = 2.0 * np.pi * n2[None, :] * (k1[:, None] + 0.25) / LENGTH
    twiddle = np.stack([np.cos(angle), -np.sin(angle)]).astype(np.float32)
    angle = 2.0 * np.pi * ((n2[:, None] * n2[None, :]) % ROWS) / ROWS
    cosine, sine = np.cos(angle), np.sin(angle)
    whole = np.block([[cosine, -sine], [sine, cosine]]).astype(np.float32)
    high = whole.astype(jnp.bfloat16)
    low = (whole - high.astype(np.float32)).astype(jnp.bfloat16)
    return twiddle, np.stack([high, low])


def times(value, angle):
    re, im = value
    turn = round(angle / (math.pi / 4), 9) % 8
    half = math.sqrt(0.5)
    if turn == 0:
        return re, im
    if turn == 2:
        return im, -re
    if turn == 1:
        return (re + im) * half, (im - re) * half
    if turn == 3:
        return (im - re) * half, -(re + im) * half
    c, s = math.cos(angle), math.sin(angle)
    return re * c + im * s, im * c - re * s


def add(a, b):
    return a[0] + b[0], a[1] + b[1]


def sub(a, b):
    return a[0] - b[0], a[1] - b[1]


def split_radix(values):
    count = len(values)
    if count == 1:
        return values
    if count == 2:
        return [add(*values), sub(*values)]
    even = split_radix(values[0::2])
    first = split_radix(values[1::4])
    third = split_radix(values[3::4])
    quarter = count // 4
    out = [None] * count
    for k in range(quarter):
        one = times(first[k], 2 * math.pi * k / count)
        two = times(third[k], 2 * math.pi * 3 * k / count)
        total, diff = add(one, two), sub(one, two)
        out[k] = add(even[k], total)
        out[k + 2 * quarter] = sub(even[k], total)
        e_re, e_im = even[k + quarter]
        out[k + quarter] = (e_re + diff[1], e_im - diff[0])
        out[k + 3 * quarter] = (e_re - diff[1], e_im + diff[0])
    return out


def pre_kernel(q_hbm, k_hbm, v_hbm, cot_hbm, taps_hbm, out_hbm, *scratch):
    buffers, out_ref, in_sems, out_sems = scratch[:5], *scratch[5:]
    sources = (q_hbm, k_hbm, v_hbm, cot_hbm, taps_hbm)
    loads = [pltpu.make_async_copy(sources[i], buffers[i], in_sems.at[i]) for i in range(5)]
    for i in (4, 1, 2, 0, 3):
        loads[i].start()
    stores = []
    for index, needs in ((2, (4,)), (0, (1, 2)), (1, (0, 3))):
        signal = None
        for i in needs:
            loads[i].wait()
            factor = buffers[i][...].astype(jnp.float32)
            signal = factor if signal is None else signal * factor
        lines = signal.T.reshape(BLOCKS, CH_EACH, ROWS)
        for s in range(BLOCKS):
            out_ref[index, PLACE[s]] = lines[s]
        here = slice(index * CH_EACH, (index + 1) * CH_EACH)
        store = pltpu.make_async_copy(
            out_ref.at[index], out_hbm.at[:, here, :], out_sems.at[index]
        )
        store.start()
        stores.append(store)
    for store in stores:
        store.wait()


def split(value):
    high = value.astype(jnp.bfloat16)
    low = (value - high.astype(jnp.float32)).astype(jnp.bfloat16)
    return high, low


def dft_rows(value, mat_ref):
    high, low = split(value)

    def dot(left, right):
        return jnp.dot(left, right, preferred_element_type=jnp.float32)

    return dot(high, mat_ref[0]) + (dot(low, mat_ref[0]) + dot(high, mat_ref[1]))


def coarse(in_ref, tw_ref, mid_ref, source, target):
    values = []
    for s in range(BLOCKS):
        signal = in_ref[PLACE[s], source, :]
        angle = 2 * math.pi * s / (4 * BLOCKS)
        values.append((signal * math.cos(angle), signal * -math.sin(angle)))
    for k1, (re, im) in enumerate(split_radix(values)):
        t_re, t_im = tw_ref[0, k1 : k1 + 1, :], tw_ref[1, k1 : k1 + 1, :]
        mid_ref[k1, target, :ROWS] = re * t_re - im * t_im
        mid_ref[k1, target, ROWS:] = re * t_im + im * t_re


def coarse_back(mid_ref, lines, scale):
    values = [(mid_ref[k1, lines, :ROWS], mid_ref[k1, lines, ROWS:]) for k1 in range(BLOCKS)]
    for s, (re, im) in enumerate(split_radix(values)):
        angle = 2 * math.pi * s / (4 * BLOCKS)
        yield s, re * (math.cos(angle) * scale) + im * (math.sin(angle) * scale)


def fine(value, mat_ref):
    groups, lines, width = value.shape
    return dft_rows(value.reshape(groups * lines, width), mat_ref).reshape(groups, lines, width)


def halves(value):
    return value[:, :, :ROWS], value[:, :, ROWS:]


def conj_times(a, b):
    (a_re, a_im), (b_re, b_im) = a, b
    return jnp.concatenate([a_re * b_re - a_im * b_im, -(a_re * b_im + a_im * b_re)], axis=2)


def conj_corr(a, b):
    (a_re, a_im), (b_re, b_im) = a, b
    return jnp.concatenate([a_re * b_re + a_im * b_im, a_re * b_im - a_im * b_re], axis=2)


def turned(value, tw_ref, here):
    re, im = halves(value)
    t_re, t_im = tw_ref[0, here, :][:, None, :], tw_ref[1, here, :][:, None, :]
    return re * t_re - im * t_im, re * t_im + im * t_re


def eight(step):
    return pl.ds(pl.multiple_of(step * 8, 8), 8)


def grad_kernel(in_ref, tw_ref, mat_ref, gain_ref, *refs):
    grad_ref, spec_ref, skip_ref, sq_ref, gain_out_ref, mid_ref, back_ref = refs
    gain_out_ref[...] = gain_ref[...]

    @pl.loop(0, 2 * CH_EACH // 8)
    def _(step):
        coarse(in_ref, tw_ref, mid_ref, eight(step), eight(step))

    @pl.loop(0, BLOCKS // GROUP)
    def _(step):
        here = pl.ds(pl.multiple_of(step * GROUP, GROUP), GROUP)
        spectrum = fine(mid_ref[here], mat_ref)
        spec_ref[here] = spectrum
        mixed, gated = halves(spectrum[:, :CH_EACH]), halves(spectrum[:, CH_EACH:])
        re, im = turned(fine(conj_corr(gated, mixed), mat_ref), tw_ref, here)
        back_ref[here, :, :ROWS] = re
        back_ref[here, :, ROWS:] = im

    time_scale = 1.0 / math.sqrt(LENGTH)
    squares = jnp.zeros((8, ROWS), jnp.float32)
    for half in range(CH_EACH // 8):
        lines = slice(half * 8, half * 8 + 8)
        for s, series in coarse_back(back_ref, lines, time_scale / LENGTH):
            grad_ref[s, lines, :] = series
            squares = squares + series * series

    direct = jnp.zeros((CH_EACH, ROWS), jnp.float32)
    for s in range(BLOCKS):
        direct = direct + in_ref[s, :CH_EACH, :] * in_ref[s, CH_EACH : 2 * CH_EACH, :]
    direct = jnp.sum(direct, axis=1, keepdims=True) * time_scale
    row = lax.broadcasted_iota(jnp.int32, (CH_EACH, ROWS), 0)
    lane = lax.broadcasted_iota(jnp.int32, (CH_EACH, ROWS), 1)
    skip = jnp.sum(jnp.where(row == lane, direct, 0.0), axis=0, keepdims=True)
    skip_ref[...] = skip
    sq_ref[...] = jnp.sum(squares, axis=0, keepdims=True) + skip * skip


def taps_kernel(in_ref, tw_ref, mat_ref, spec_ref, mid_ref):
    @pl.loop(0, CH_EACH // 8)
    def _(step):
        source = pl.ds(pl.multiple_of(step * 8 + 2 * CH_EACH, 8), 8)
        coarse(in_ref, tw_ref, mid_ref, source, eight(step))

    @pl.loop(0, BLOCKS // WIDER)
    def _(step):
        here = pl.ds(pl.multiple_of(step * WIDER, WIDER), WIDER)
        spec_ref[here] = fine(mid_ref[here], mat_ref)


def conv_kernel(line, combine, spec_ref, taps_ref, tw_ref, mat_ref, after_ref, out_ref, mid_ref):
    @pl.loop(0, BLOCKS // WIDER)
    def _(step):
        here = pl.ds(pl.multiple_of(step * WIDER, WIDER), WIDER)
        signal = halves(spec_ref[here, line : line + CH_EACH])
        product = combine(signal, halves(taps_ref[here]))
        re, im = turned(fine(product, mat_ref), tw_ref, here)
        mid_ref[here, :, :ROWS] = re
        mid_ref[here, :, ROWS:] = im

    for first in range(0, CH_EACH, 8):
        lines = slice(first, first + 8)
        for s, series in coarse_back(mid_ref, lines, 1.0 / LENGTH):
            out_ref[s, lines, :] = series


def pack_kernel(conv_ref, back_ref, grad_ref, skip_ref, one_ref, two_ref, out_ref):
    squares = jnp.sum(one_ref[...] + two_ref[...], axis=1, keepdims=True)
    lane = lax.broadcasted_iota(jnp.int32, (1, ROWS), 1)
    last = jnp.where(lane == CH_EACH, squares, skip_ref[...])
    for s in range(BLOCKS):
        first = PLACE[s] * BACK
        for ref in (conv_ref, back_ref, grad_ref):
            out_ref[first : first + CH_EACH, :] = ref[s]
            first += CH_EACH
        out_ref[first : first + 1, :] = last


def statistics(in_ref, skip_ref, rms_ref, count):
    per_row = ROWS // CH_EACH
    rows = BLOCKS // per_row
    lane = lax.broadcasted_iota(jnp.int32, (rows, ROWS), 1)
    skip = jnp.zeros((rows, ROWS), jnp.float32)
    squares = jnp.zeros((rows, ROWS), jnp.float32)
    for m in range(per_row):
        at = [PLACE[r * per_row + m] * BACK + LINES for r in range(rows)]
        lines = jnp.concatenate([in_ref[i : i + 1, :] for i in at], axis=0)
        squares = squares + jnp.where(lane == CH_EACH, lines, 0.0)
        moved = pltpu.roll(lines, m * CH_EACH, 1) if m else lines
        skip = jnp.where(lane // CH_EACH == m, moved, skip)
    skip_ref[...] = skip
    total = jnp.sum(jnp.sum(squares, axis=0, keepdims=True), axis=1, keepdims=True)
    rms_ref[...] = jnp.sqrt(total * (1.0 / count))


def post_kernel(count, in_ref, q_ref, k_ref, v_ref, cot_ref, gain_ref, *outs):
    out_ref, dq_ref, dk_ref, dv_ref, dh_ref, skip_ref, rms_ref = outs
    statistics(in_ref, skip_ref, rms_ref, count)

    def series(index):
        first = [PLACE[s] * BACK + index * CH_EACH for s in range(BLOCKS)]
        return jnp.concatenate([in_ref[i : i + CH_EACH, :] for i in first], axis=0).T

    query = q_ref[...].astype(jnp.float32)
    key = k_ref[...].astype(jnp.float32)
    value = v_ref[...].astype(jnp.float32)
    cot = cot_ref[...].astype(jnp.float32)
    gain = gain_ref[...]
    inner = series(0) + gain * (key * value)
    out_ref[...] = (query * inner).astype(jnp.bfloat16)
    dq_ref[...] = (cot * inner).astype(jnp.bfloat16)
    mixed_grad = series(1) + gain * (query * cot)
    dk_ref[...] = (mixed_grad * value).astype(jnp.bfloat16)
    dv_ref[...] = (mixed_grad * key).astype(jnp.bfloat16)
    dh_ref[...] = series(2)


def partner(array, bit):
    return lax.ppermute(array, "ch", [(i, i ^ bit) for i in range(lax.axis_size("ch"))])


def exchange(array):
    return lax.all_to_all(array, "seq", 0, 0, axis_index_groups=[ORDER], tiled=True)


def f32(*shape):
    return jax.ShapeDtypeStruct(shape, jnp.float32)


PARAMS = pltpu.CompilerParams(vmem_limit_bytes=40 * 2**20)
COST = pl.CostEstimate(flops=2 * 10**9, bytes_accessed=4 * 10**6, transcendentals=0)
WIDE = pltpu.CompilerParams(vmem_limit_bytes=60 * 2**20)


def body(query, key, value, cotangent, taps, gain):
    rows, channels = query.shape
    twiddle, matrix = tables()
    signals = (query, key, value, cotangent, taps)
    hbm = pl.BlockSpec(memory_space=pltpu.HBM)
    packed = pl.pallas_call(
        pre_kernel,
        out_shape=f32(BLOCKS, LINES, ROWS),
        in_specs=[hbm] * len(signals),
        out_specs=hbm,
        scratch_shapes=[pltpu.VMEM(signal.shape, signal.dtype) for signal in signals]
        + [
            pltpu.VMEM((3, BLOCKS, CH_EACH, ROWS), jnp.float32),
            pltpu.SemaphoreType.DMA((len(signals),)),
            pltpu.SemaphoreType.DMA((3,)),
        ],
        compiler_params=WIDE,
    )(*signals)
    lines = exchange(packed)
    room = functools.partial(pltpu.VMEM, dtype=jnp.float32)
    grad, spectra, skip_part, squares, gain = pl.pallas_call(
        grad_kernel,
        out_shape=(
            f32(BLOCKS, CH_EACH, ROWS),
            f32(BLOCKS, 2 * CH_EACH, 2 * ROWS),
            f32(1, ROWS),
            f32(1, ROWS),
            f32(1, channels),
        ),
        scratch_shapes=[
            room((BLOCKS, 2 * CH_EACH, 2 * ROWS)),
            room((BLOCKS, CH_EACH, 2 * ROWS)),
        ],
        compiler_params=PARAMS,
        cost_estimate=COST,
    )(lines, twiddle, matrix, gain[None, :])
    squares = squares + partner(squares, 1)
    taps_spectrum = pl.pallas_call(
        taps_kernel,
        out_shape=f32(BLOCKS, CH_EACH, 2 * ROWS),
        scratch_shapes=[room((BLOCKS, CH_EACH, 2 * ROWS))],
        compiler_params=PARAMS,
        cost_estimate=COST,
    )(lines, twiddle, matrix)

    def convolution(line, combine, after):
        return pl.pallas_call(
            functools.partial(conv_kernel, line, combine),
            out_shape=f32(BLOCKS, CH_EACH, ROWS),
            scratch_shapes=[room((BLOCKS, CH_EACH, 2 * ROWS))],
            compiler_params=PARAMS,
            cost_estimate=COST,
        )(spectra, taps_spectrum, twiddle, matrix, after)

    conv = convolution(0, conj_times, squares)
    squares = squares + partner(squares, 2)
    back = convolution(CH_EACH, conj_corr, squares)
    returned = pl.pallas_call(
        pack_kernel,
        out_shape=f32(BLOCKS * BACK, ROWS),
        compiler_params=PARAMS,
    )(conv, back, grad, skip_part, squares, partner(squares, 6))
    returned = exchange(returned.reshape(BLOCKS, BACK, 1, ROWS)).reshape(BLOCKS * BACK, ROWS)
    bf16 = jax.ShapeDtypeStruct((rows, channels), jnp.bfloat16)
    count = channels * lax.axis_size("ch") * (LENGTH + 1)
    *outputs, skip_grad, grad_rms = pl.pallas_call(
        functools.partial(post_kernel, count),
        out_shape=(
            *[bf16] * 4,
            f32(rows, channels),
            f32(channels // ROWS, ROWS),
            f32(1, 1),
        ),
        compiler_params=PARAMS,
    )(returned, query, key, value, cotangent, gain)
    return (*outputs, skip_grad.reshape(channels), grad_rms[0, 0])


def solution(mesh):
    both = P("seq", "ch")
    return jax.shard_map(
        body,
        mesh=mesh,
        in_specs=(both, both, both, both, both, P("ch")),
        out_specs=(both, both, both, both, both, P("ch"), P()),
        check_vma=False,
    )
```

```python
import functools
import math

import jax
import jax.numpy as jnp
import numpy as np
from jax import lax
from jax.experimental import pallas as pl
from jax.experimental.pallas import tpu as pltpu
from jax.sharding import PartitionSpec as P

ROWS = 128
BLOCKS = 32
LENGTH = ROWS * BLOCKS
CH_EACH = 16
LINES = 3 * CH_EACH
GROUP = 32
WIDER = 32
BACK = LINES + 1
ORDER = [
    23, 20, 27, 29, 10, 22, 12, 1, 0, 24, 28, 19, 6, 18, 21, 11,
    2, 31, 16, 26, 5, 15, 3, 17, 8, 30, 14, 25, 7, 13, 9, 4,
]
PLACE = [ORDER.index(s) for s in range(BLOCKS)]


def tables():
    n2 = np.arange(ROWS)
    k1 = np.arange(BLOCKS)
    angle = 2.0 * np.pi * n2[None, :] * (k1[:, None] + 0.25) / LENGTH
    twiddle = np.stack([np.cos(angle), -np.sin(angle)]).astype(np.float32)
    angle = 2.0 * np.pi * ((n2[:, None] * n2[None, :]) % ROWS) / ROWS
    cosine, sine = np.cos(angle), np.sin(angle)
    whole = np.block([[cosine, -sine], [sine, cosine]]).astype(np.float32)
    high = whole.astype(jnp.bfloat16)
    low = (whole - high.astype(np.float32)).astype(jnp.bfloat16)
    return twiddle, np.stack([high, low])


def times(value, angle):
    re, im = value
    turn = round(angle / (math.pi / 4), 9) % 8
    half = math.sqrt(0.5)
    if turn == 0:
        return re, im
    if turn == 2:
        return im, -re
    if turn == 1:
        return (re + im) * half, (im - re) * half
    if turn == 3:
        return (im - re) * half, -(re + im) * half
    c, s = math.cos(angle), math.sin(angle)
    return re * c + im * s, im * c - re * s


def add(a, b):
    return a[0] + b[0], a[1] + b[1]


def sub(a, b):
    return a[0] - b[0], a[1] - b[1]


def split_radix(values):
    count = len(values)
    if count == 1:
        return values
    if count == 2:
        return [add(*values), sub(*values)]
    even = split_radix(values[0::2])
    first = split_radix(values[1::4])
    third = split_radix(values[3::4])
    quarter = count // 4
    out = [None] * count
    for k in range(quarter):
        one = times(first[k], 2 * math.pi * k / count)
        two = times(third[k], 2 * math.pi * 3 * k / count)
        total, diff = add(one, two), sub(one, two)
        out[k] = add(even[k], total)
        out[k + 2 * quarter] = sub(even[k], total)
        e_re, e_im = even[k + quarter]
        out[k + quarter] = (e_re + diff[1], e_im - diff[0])
        out[k + 3 * quarter] = (e_re - diff[1], e_im + diff[0])
    return out


def pre_kernel(q_hbm, k_hbm, v_hbm, cot_hbm, taps_hbm, out_hbm, *scratch):
    buffers, out_ref, in_sems, out_sems = scratch[:5], *scratch[5:]
    sources = (q_hbm, k_hbm, v_hbm, cot_hbm, taps_hbm)
    loads = [pltpu.make_async_copy(sources[i], buffers[i], in_sems.at[i]) for i in range(5)]
    for i in (4, 1, 2, 0, 3):
        loads[i].start()
    stores = []
    for index, needs in ((2, (4,)), (0, (1, 2)), (1, (0, 3))):
        signal = None
        for i in needs:
            loads[i].wait()
            factor = buffers[i][...].astype(jnp.float32)
            signal = factor if signal is None else signal * factor
        lines = signal.T.reshape(BLOCKS, CH_EACH, ROWS)
        for s in range(BLOCKS):
            out_ref[index, PLACE[s]] = lines[s]
        here = slice(index * CH_EACH, (index + 1) * CH_EACH)
        store = pltpu.make_async_copy(
            out_ref.at[index], out_hbm.at[:, here, :], out_sems.at[index]
        )
        store.start()
        stores.append(store)
    for store in stores:
        store.wait()


def split(value):
    high = value.astype(jnp.bfloat16)
    low = (value - high.astype(jnp.float32)).astype(jnp.bfloat16)
    return high, low


def dft_rows(value, mat_ref):
    high, low = split(value)

    def dot(left, right):
        return jnp.dot(left, right, preferred_element_type=jnp.float32)

    return dot(high, mat_ref[0]) + (dot(low, mat_ref[0]) + dot(high, mat_ref[1]))


def coarse(in_ref, tw_ref, mid_ref, source, target):
    values = []
    for s in range(BLOCKS):
        signal = in_ref[PLACE[s], source, :]
        angle = 2 * math.pi * s / (4 * BLOCKS)
        values.append((signal * math.cos(angle), signal * -math.sin(angle)))
    for k1, (re, im) in enumerate(split_radix(values)):
        t_re, t_im = tw_ref[0, k1 : k1 + 1, :], tw_ref[1, k1 : k1 + 1, :]
        mid_ref[k1, target, :ROWS] = re * t_re - im * t_im
        mid_ref[k1, target, ROWS:] = re * t_im + im * t_re


def coarse_back(mid_ref, lines, scale):
    values = [(mid_ref[k1, lines, :ROWS], mid_ref[k1, lines, ROWS:]) for k1 in range(BLOCKS)]
    for s, (re, im) in enumerate(split_radix(values)):
        angle = 2 * math.pi * s / (4 * BLOCKS)
        yield s, re * (math.cos(angle) * scale) + im * (math.sin(angle) * scale)


def fine(value, mat_ref):
    groups, lines, width = value.shape
    return dft_rows(value.reshape(groups * lines, width), mat_ref).reshape(groups, lines, width)


def halves(value):
    return value[:, :, :ROWS], value[:, :, ROWS:]


def conj_times(a, b):
    (a_re, a_im), (b_re, b_im) = a, b
    return jnp.concatenate([a_re * b_re - a_im * b_im, -(a_re * b_im + a_im * b_re)], axis=2)


def conj_corr(a, b):
    (a_re, a_im), (b_re, b_im) = a, b
    return jnp.concatenate([a_re * b_re + a_im * b_im, a_re * b_im - a_im * b_re], axis=2)


def turned(value, tw_ref, here):
    re, im = halves(value)
    t_re, t_im = tw_ref[0, here, :][:, None, :], tw_ref[1, here, :][:, None, :]
    return re * t_re - im * t_im, re * t_im + im * t_re


def eight(step):
    return pl.ds(pl.multiple_of(step * 8, 8), 8)


def grad_kernel(in_ref, tw_ref, mat_ref, gain_ref, *refs):
    grad_ref, spec_ref, skip_ref, sq_ref, gain_out_ref, mid_ref, back_ref = refs
    gain_out_ref[...] = gain_ref[...]

    @pl.loop(0, 2 * CH_EACH // 8)
    def _(step):
        coarse(in_ref, tw_ref, mid_ref, eight(step), eight(step))

    @pl.loop(0, BLOCKS // GROUP)
    def _(step):
        here = pl.ds(pl.multiple_of(step * GROUP, GROUP), GROUP)
        spectrum = fine(mid_ref[here], mat_ref)
        spec_ref[here] = spectrum
        mixed, gated = halves(spectrum[:, :CH_EACH]), halves(spectrum[:, CH_EACH:])
        re, im = turned(fine(conj_corr(gated, mixed), mat_ref), tw_ref, here)
        back_ref[here, :, :ROWS] = re
        back_ref[here, :, ROWS:] = im

    time_scale = 1.0 / math.sqrt(LENGTH)
    squares = jnp.zeros((8, ROWS), jnp.float32)
    for half in range(CH_EACH // 8):
        lines = slice(half * 8, half * 8 + 8)
        for s, series in coarse_back(back_ref, lines, time_scale / LENGTH):
            grad_ref[s, lines, :] = series
            squares = squares + series * series

    direct = jnp.zeros((CH_EACH, ROWS), jnp.float32)
    for s in range(BLOCKS):
        direct = direct + in_ref[s, :CH_EACH, :] * in_ref[s, CH_EACH : 2 * CH_EACH, :]
    direct = jnp.sum(direct, axis=1, keepdims=True) * time_scale
    row = lax.broadcasted_iota(jnp.int32, (CH_EACH, ROWS), 0)
    lane = lax.broadcasted_iota(jnp.int32, (CH_EACH, ROWS), 1)
    skip = jnp.sum(jnp.where(row == lane, direct, 0.0), axis=0, keepdims=True)
    skip_ref[...] = skip
    sq_ref[...] = jnp.sum(squares, axis=0, keepdims=True) + skip * skip


def taps_kernel(in_ref, tw_ref, mat_ref, spec_ref, mid_ref):
    @pl.loop(0, CH_EACH // 8)
    def _(step):
        source = pl.ds(pl.multiple_of(step * 8 + 2 * CH_EACH, 8), 8)
        coarse(in_ref, tw_ref, mid_ref, source, eight(step))

    @pl.loop(0, BLOCKS // WIDER)
    def _(step):
        here = pl.ds(pl.multiple_of(step * WIDER, WIDER), WIDER)
        spec_ref[here] = fine(mid_ref[here], mat_ref)


def conv_kernel(line, combine, spec_ref, taps_ref, tw_ref, mat_ref, after_ref, out_ref, mid_ref):
    @pl.loop(0, BLOCKS // WIDER)
    def _(step):
        here = pl.ds(pl.multiple_of(step * WIDER, WIDER), WIDER)
        signal = halves(spec_ref[here, line : line + CH_EACH])
        product = combine(signal, halves(taps_ref[here]))
        re, im = turned(fine(product, mat_ref), tw_ref, here)
        mid_ref[here, :, :ROWS] = re
        mid_ref[here, :, ROWS:] = im

    for first in range(0, CH_EACH, 8):
        lines = slice(first, first + 8)
        for s, series in coarse_back(mid_ref, lines, 1.0 / LENGTH):
            out_ref[s, lines, :] = series


def pack_kernel(conv_ref, back_ref, grad_ref, skip_ref, one_ref, two_ref, out_ref):
    squares = jnp.sum(one_ref[...] + two_ref[...], axis=1, keepdims=True)
    lane = lax.broadcasted_iota(jnp.int32, (1, ROWS), 1)
    last = jnp.where(lane == CH_EACH, squares, skip_ref[...])
    for s in range(BLOCKS):
        first = PLACE[s] * BACK
        for ref in (conv_ref, back_ref, grad_ref):
            out_ref[first : first + CH_EACH, :] = ref[s]
            first += CH_EACH
        out_ref[first : first + 1, :] = last


def statistics(in_ref, skip_ref, rms_ref, count):
    per_row = ROWS // CH_EACH
    rows = BLOCKS // per_row
    lane = lax.broadcasted_iota(jnp.int32, (rows, ROWS), 1)
    skip = jnp.zeros((rows, ROWS), jnp.float32)
    squares = jnp.zeros((rows, ROWS), jnp.float32)
    for m in range(per_row):
        at = [PLACE[r * per_row + m] * BACK + LINES for r in range(rows)]
        lines = jnp.concatenate([in_ref[i : i + 1, :] for i in at], axis=0)
        squares = squares + jnp.where(lane == CH_EACH, lines, 0.0)
        moved = pltpu.roll(lines, m * CH_EACH, 1) if m else lines
        skip = jnp.where(lane // CH_EACH == m, moved, skip)
    skip_ref[...] = skip
    total = jnp.sum(jnp.sum(squares, axis=0, keepdims=True), axis=1, keepdims=True)
    rms_ref[...] = jnp.sqrt(total * (1.0 / count))


def post_kernel(count, in_ref, q_ref, k_ref, v_ref, cot_ref, gain_ref, *outs):
    hbm, (skip_ref, rms_ref), held, sems = outs[:5], outs[5:7], outs[7:12], outs[12]
    stores = []

    def store(index, result):
        held[index][...] = result
        copy = pltpu.make_async_copy(held[index], hbm[index], sems.at[index])
        copy.start()
        stores.append(copy)

    def series(index):
        first = [PLACE[s] * BACK + index * CH_EACH for s in range(BLOCKS)]
        return jnp.concatenate([in_ref[i : i + CH_EACH, :] for i in first], axis=0).T

    store(4, series(2))
    query = q_ref[...].astype(jnp.float32)
    key = k_ref[...].astype(jnp.float32)
    value = v_ref[...].astype(jnp.float32)
    cot = cot_ref[...].astype(jnp.float32)
    gain = gain_ref[...]
    inner = series(0) + gain * (key * value)
    store(0, (query * inner).astype(jnp.bfloat16))
    store(1, (cot * inner).astype(jnp.bfloat16))
    mixed_grad = series(1) + gain * (query * cot)
    store(2, (mixed_grad * value).astype(jnp.bfloat16))
    store(3, (mixed_grad * key).astype(jnp.bfloat16))
    statistics(in_ref, skip_ref, rms_ref, count)
    for copy in stores:
        copy.wait()


def partner(array, bit):
    return lax.ppermute(array, "ch", [(i, i ^ bit) for i in range(lax.axis_size("ch"))])


def exchange(array):
    return lax.all_to_all(array, "seq", 0, 0, axis_index_groups=[ORDER], tiled=True)


def f32(*shape):
    return jax.ShapeDtypeStruct(shape, jnp.float32)


PARAMS = pltpu.CompilerParams(vmem_limit_bytes=40 * 2**20)
COST = pl.CostEstimate(flops=2 * 10**9, bytes_accessed=4 * 10**6, transcendentals=0)
WIDE = pltpu.CompilerParams(vmem_limit_bytes=60 * 2**20)


def body(query, key, value, cotangent, taps, gain):
    rows, channels = query.shape
    twiddle, matrix = tables()
    signals = (query, key, value, cotangent, taps)
    hbm = pl.BlockSpec(memory_space=pltpu.HBM)
    packed = pl.pallas_call(
        pre_kernel,
        out_shape=f32(BLOCKS, LINES, ROWS),
        in_specs=[hbm] * len(signals),
        out_specs=hbm,
        scratch_shapes=[pltpu.VMEM(signal.shape, signal.dtype) for signal in signals]
        + [
            pltpu.VMEM((3, BLOCKS, CH_EACH, ROWS), jnp.float32),
            pltpu.SemaphoreType.DMA((len(signals),)),
            pltpu.SemaphoreType.DMA((3,)),
        ],
        compiler_params=WIDE,
    )(*signals)
    lines = exchange(packed)
    room = functools.partial(pltpu.VMEM, dtype=jnp.float32)
    grad, spectra, skip_part, squares, gain = pl.pallas_call(
        grad_kernel,
        out_shape=(
            f32(BLOCKS, CH_EACH, ROWS),
            f32(BLOCKS, 2 * CH_EACH, 2 * ROWS),
            f32(1, ROWS),
            f32(1, ROWS),
            f32(1, channels),
        ),
        scratch_shapes=[
            room((BLOCKS, 2 * CH_EACH, 2 * ROWS)),
            room((BLOCKS, CH_EACH, 2 * ROWS)),
        ],
        compiler_params=PARAMS,
        cost_estimate=COST,
    )(lines, twiddle, matrix, gain[None, :])
    squares = squares + partner(squares, 1)
    taps_spectrum = pl.pallas_call(
        taps_kernel,
        out_shape=f32(BLOCKS, CH_EACH, 2 * ROWS),
        scratch_shapes=[room((BLOCKS, CH_EACH, 2 * ROWS))],
        compiler_params=PARAMS,
        cost_estimate=COST,
    )(lines, twiddle, matrix)

    def convolution(line, combine, after):
        return pl.pallas_call(
            functools.partial(conv_kernel, line, combine),
            out_shape=f32(BLOCKS, CH_EACH, ROWS),
            scratch_shapes=[room((BLOCKS, CH_EACH, 2 * ROWS))],
            compiler_params=PARAMS,
            cost_estimate=COST,
        )(spectra, taps_spectrum, twiddle, matrix, after)

    conv = convolution(0, conj_times, squares)
    squares = squares + partner(squares, 2)
    back = convolution(CH_EACH, conj_corr, squares)
    returned = pl.pallas_call(
        pack_kernel,
        out_shape=f32(BLOCKS * BACK, ROWS),
        compiler_params=PARAMS,
    )(conv, back, grad, skip_part, squares, partner(squares, 6))
    returned = exchange(returned.reshape(BLOCKS, BACK, 1, ROWS)).reshape(BLOCKS * BACK, ROWS)
    bf16 = jax.ShapeDtypeStruct((rows, channels), jnp.bfloat16)
    count = channels * lax.axis_size("ch") * (LENGTH + 1)
    *outputs, skip_grad, grad_rms = pl.pallas_call(
        functools.partial(post_kernel, count),
        out_shape=(
            *[bf16] * 4,
            f32(rows, channels),
            f32(channels // ROWS, ROWS),
            f32(1, 1),
        ),
        out_specs=(*[hbm] * 5, *[pl.BlockSpec(memory_space=pltpu.VMEM)] * 2),
        scratch_shapes=[pltpu.VMEM((rows, channels), jnp.bfloat16)] * 4
        + [pltpu.VMEM((rows, channels), jnp.float32), pltpu.SemaphoreType.DMA((5,))],
        compiler_params=PARAMS,
    )(returned, query, key, value, cotangent, gain)
    return (*outputs, skip_grad.reshape(channels), grad_rms[0, 0])


def solution(mesh):
    both = P("seq", "ch")
    return jax.shard_map(
        body,
        mesh=mesh,
        in_specs=(both, both, both, both, both, P("ch")),
        out_specs=(both, both, both, both, both, P("ch"), P()),
        check_vma=False,
    )
```
